512 devices in a mesh: leaf: 64 (over z, y), oct: 8 (over x, core).
Axes of the slice: x: 4, y: 4, z: 16, core: 2. Of those that a mesh axis runs over, the one named last changes fastest.
Arguments:
- children: bfloat16 [16384, 4096], P(('leaf', 'oct')), may hold values from -6 to 6
- child_slot: int32 [2048, 8], P('leaf', 'oct'), may hold values from 0 to 31, as said below
- two_scale: bfloat16 [32, 32], replicated, may hold values from -1 to 1
- factors: bfloat16 [27, 30720], replicated, may hold values from -0.5390625 to 0.5390625
- disp_kind: int32 [2048, 4], P(('leaf', 'oct')), may hold values from 0 to 26
- target_leaf: int32 [2048, 4, 1], P(('leaf', 'oct')), may hold values from 0 to 63; in each aligned block of 16 rows (0 to 15, 16 to 31, ..., all dimensions but the last counted through in order) at most 2 rows name the same one
- target_node: int32 [2048, 4], P(('leaf', 'oct')), may hold values from 0 to 15
Outputs:
- octant_out: bfloat16 [1024, 8, 4096], P('leaf', 'oct')
The draws below stay inside these ranges and needn't reach their ends.
Inputs may be any that keep to these rules, and one draw needn't show every extreme that they name: Over the parents of one subtree and the octants held by one device along oct, child_slot takes every value exactly once. `target_leaf`: of the 16 entries of one device, at most 2 name the same subtree; some device reaches 2.
All inputs are finite; a program needn't handle non-finite values.
Results may differ from the reference program's by a relative error of at most 0.018.
Values may be sent and summed in bfloat16 or wider, within the bound.
A program may use at most 64 MiB of HBM per device.

```python
import math
import jax
import jax.numpy as jnp
import numpy as np
from jax import lax

K = 16
TERMS = 10
DISPS = 4
KINDS = 27
PAR_DEV = 4
TGT_DEV = 2
PARENTS = 2048
BLOCKS = 16384
TARGETS = 1024
CAP = 2
N_LEAF = 64
N_OCT = 8


def draw_child_slot(key, part):
    group_size = PAR_DEV * N_OCT
    held_octants = 8 // N_OCT
    block_total = PAR_DEV * 8
    device_keys = jax.random.split(jax.random.fold_in(key, 17), N_LEAF * N_OCT)
    shuffled = jax.vmap(lambda one_key: jax.random.permutation(one_key, block_total))(device_keys)
    shuffled = shuffled.reshape(N_LEAF, N_OCT, group_size, held_octants)
    shuffled = jnp.transpose(shuffled, (0, 2, 1, 3)).reshape(N_LEAF * group_size, 8)
    return shuffled.astype(jnp.int32)


def plant(array, stream_key, smallest, high):
    spot = [jax.random.randint(jax.random.fold_in(stream_key, axis), (), 0, length) for axis, length in enumerate(array.shape)]
    longest = array.shape.index(max(array.shape))
    next_to = spot[:longest] + [(spot[longest] + 1) % array.shape[longest]] + spot[longest + 1:]
    return array.at[tuple(spot)].set(smallest).at[tuple(next_to)].set(high)


def level_of(stream_key, shape, cuts, low, high):
    loudness = 1.0
    for position, blocks in cuts:
        draws = jax.random.uniform(jax.random.fold_in(jax.random.fold_in(stream_key, 6), position), (blocks,), jnp.float32, low / len(cuts), high / len(cuts))
        loudness = loudness * jnp.repeat(jnp.exp(draws), shape[position] // blocks).reshape((-1,) + (1,) * (len(shape) - 1 - position))
    return loudness


def deal_out(own_key, own, number, rows, count, top, bound, slope):
    order = jax.random.permutation(own_key, count)
    packed, usual = portions_of(count, rows * top, bound, slope, True), portions_of(count, rows * top, bound, slope, False)
    places = jnp.arange(count)

    def named(sizes, offset_by):
        used = int((sizes > 0).sum())
        fixed = max(1, used // 4)
        shifted = fixed + (places - fixed + offset_by * (used - fixed)) % max(1, count - fixed)
        return jnp.zeros((count,), jnp.int32).at[order[jnp.where(places < fixed, places, shifted)]].set(jnp.asarray(sizes, jnp.int32))

    sizes = jnp.where(number % 4 == 0, named(packed, number // 4), named(usual, number - number // 4 - 1))
    mixed = jax.random.permutation(jax.random.fold_in(own, 3), count)
    donor, taker = mixed[0:count // 2 * 2:2], mixed[1:count // 2 * 2:2]
    margin = jnp.minimum(sizes[donor] - 1, bound - sizes[taker]) // 2
    margin = jnp.where((donor == order[0]) | (taker == order[0]) | (sizes[taker] == 0), 0, jnp.maximum(margin, 0))
    shifted = jax.random.randint(jax.random.fold_in(own, 4), (count // 2,), 0, 1 << 20) % (margin + 1)
    sizes = sizes.at[donor].add(-shifted).at[taker].add(shifted)
    items = jnp.searchsorted(jnp.cumsum(sizes), jnp.arange(rows * top), side="right").astype(jnp.int32)
    table = items.reshape(top, rows).T
    table = table[jax.random.permutation(jax.random.fold_in(own, 1), rows)]
    offset_by = jax.random.randint(jax.random.fold_in(own, 2), (rows, 1), 0, top)
    return jnp.take_along_axis(table, (jnp.arange(top)[None, :] + offset_by) % top, axis=1)


def portions_of(count, total, bound, slope, full):
    loads = [(1 << 20) // math.isqrt(standing ** slope) + 1 for standing in range(1, count + 1)]
    largest = bound if full else min(bound, max(-(-total // count), total * loads[0] // sum(loads)))
    least = 1 if total - largest >= count - 1 else 0
    given, surplus = [largest] + [least] * (count - 1), total - largest - least * (count - 1)
    while surplus > 0:
        movable = [i for i in range(1, count) if given[i] < largest] or [i for i in range(1, count) if given[i] < bound]
        pool, budget = sum([loads[i] for i in movable]), surplus
        for i in movable:
            addition = min(bound - given[i], max(1, budget * loads[i] // pool), surplus)
            given[i] = given[i] + addition
            surplus = surplus - addition
    return np.array(given)


def bell_draw(rng, extent, spread, limit, cuts=(), kind=jnp.bfloat16):
    values = spread * jax.random.normal(rng, extent, jnp.float32)
    if cuts:
        values = values * level_of(rng, extent, cuts, -0.22, 0.18)
    return jnp.clip(values, -limit, limit).astype(kind)


def setup_inputs(seed: int = 0) -> dict:
    keys = jax.random.split(jax.random.key(seed), 8)
    children = bell_draw(keys[0], (BLOCKS, K * K * K), 1.0, 6.0, ((0, 512),))
    child_slot = draw_child_slot(jax.random.fold_in(keys[7], 71), 0)
    two_scale = bell_draw(keys[2], (2 * K, 2 * K), (2 * K) ** -0.5, 1.0)
    factors = bell_draw(keys[3], (KINDS, 3 * TERMS * 4 * K * K), 0.09, 0.5390625)
    disp_kind = plant(jax.random.randint(keys[4], (PARENTS, DISPS), 0, KINDS), jax.random.fold_in(keys[4], 1), 0, KINDS - 1).astype(jnp.int32)
    target_leaf_keys = jax.random.split(jax.random.fold_in(keys[5], 1), PARENTS * DISPS // (PAR_DEV * DISPS))
    target_leaf_turns = jax.random.permutation(jax.random.fold_in(keys[5], 3), PARENTS * DISPS // (PAR_DEV * DISPS))
    target_leaf = jax.vmap(lambda own, number: deal_out(jax.random.fold_in(keys[5], 2), own, number, PAR_DEV * DISPS, N_LEAF, 1, CAP, 2))(target_leaf_keys, target_leaf_turns).reshape((PARENTS, DISPS, 1))
    target_node = plant(jax.random.randint(keys[6], (PARENTS, DISPS), 0, TGT_DEV * N_OCT), jax.random.fold_in(keys[6], 1), 0, (TGT_DEV * N_OCT) - 1).astype(jnp.int32)
    return {"children": children, "child_slot": child_slot, "two_scale": two_scale, "factors": factors, "disp_kind": disp_kind, "target_leaf": target_leaf, "target_node": target_node}


def filter_blocks(block_batch, filter_halfset):
    half_edge = filter_halfset.shape[2]
    count_batch = block_batch.shape[0]
    split_blocks = block_batch.reshape(count_batch, 2, 2, 2, half_edge, half_edge, half_edge).astype(jnp.float32)
    halfset_width = filter_halfset.astype(jnp.float32)
    first_pass = jnp.einsum('nijlpsr,aip->najlsr', split_blocks, halfset_width).astype(jnp.bfloat16)
    second_sweep = jnp.einsum('najlsr,bjs->nablr', first_pass.astype(jnp.float32), halfset_width).astype(jnp.bfloat16)
    third_sweep = jnp.einsum('qyixz,wxz->qyiw', second_sweep.astype(jnp.float32), halfset_width).astype(jnp.bfloat16)
    return third_sweep


def unfilter_blocks(cube_batch, filter_halfset):
    half_edge = filter_halfset.shape[2]
    count_batch = cube_batch.shape[0]
    halfset_width = filter_halfset.astype(jnp.float32)
    first_pass = jnp.einsum('nabc,aip->nipbc', cube_batch.astype(jnp.float32), halfset_width).astype(jnp.bfloat16)
    second_sweep = jnp.einsum('nipbc,bjs->nipjsc', first_pass.astype(jnp.float32), halfset_width).astype(jnp.bfloat16)
    third_sweep = jnp.einsum('xmezhw,wbf->xmezhbf', second_sweep.astype(jnp.float32), halfset_width).astype(jnp.bfloat16)
    ordered = jnp.transpose(third_sweep, (0, 1, 3, 5, 2, 4, 6))
    return ordered.reshape(count_batch, 8, half_edge * half_edge * half_edge)


def apply_parent(parent_cube, factor_set):
    cube_wide = parent_cube.astype(jnp.float32)
    factor_wide = factor_set.astype(jnp.float32)
    section_z = jnp.einsum('abc,ktdc->ktabd', cube_wide, factor_wide[:, 2]).astype(jnp.bfloat16)
    section_y = jnp.einsum('ktabd,kteb->ktaed', section_z.astype(jnp.float32), factor_wide[:, 1]).astype(jnp.bfloat16)
    summed = jnp.einsum('ktaed,ktfa->kfed', section_y.astype(jnp.float32), factor_wide[:, 0]).astype(jnp.bfloat16)
    return summed.reshape(summed.shape[0], -1)


def reference(children, child_slot, two_scale, factors, disp_kind, target_leaf, target_node):
    edge_len = 2 * K
    group_size = PAR_DEV * N_OCT
    held_octants = 8 // N_OCT
    node_count = TGT_DEV * N_OCT
    filter_halfset = two_scale.reshape(edge_len, 2, K)
    factor_table = factors.reshape(KINDS, 3, TERMS, edge_len, edge_len)
    parent_ids = jnp.arange(PARENTS, dtype=jnp.int32)
    octant_ids = jnp.arange(8, dtype=jnp.int32)
    owner_device = (parent_ids[:, None] // group_size) * N_OCT + octant_ids[None, :] // held_octants
    block_rows = (owner_device * (8 * PAR_DEV) + child_slot).astype(jnp.int32)
    goal_nodes = (target_leaf[:, :, 0] * node_count + target_node).astype(jnp.int32)

    def scan_step(node_totals, scan_item):
        block_row, kind_index, goal_node = scan_item
        picked_blocks = children[block_row]
        parent_cube = filter_blocks(picked_blocks[None], filter_halfset)[0]
        contribution = apply_parent(parent_cube, factor_table[kind_index])
        return node_totals.at[goal_node].add(contribution.astype(jnp.float32)), None

    start_totals = jnp.zeros((TARGETS, edge_len * edge_len * edge_len), jnp.float32)
    node_totals, unused_out = lax.scan(scan_step, start_totals, (block_rows, disp_kind, goal_nodes))
    target_blocks = node_totals.astype(jnp.bfloat16).reshape(TARGETS, edge_len, edge_len, edge_len)
    return lax.map(lambda single_cube: unfilter_blocks(single_cube[None], filter_halfset)[0], target_blocks)
```

```python
import functools

import jax
import jax.numpy as jnp
from jax import lax
from jax.experimental import pallas as pl
from jax.experimental.pallas import tpu as pltpu
from jax.sharding import PartitionSpec as P

BF = jnp.bfloat16
F32 = jnp.float32
MESH = pl.DeviceIdType.MESH
VM = pl.BlockSpec(memory_space=pltpu.VMEM)
NT = (((1,), (1,)), ((), ()))
NN = (((1,), (0,)), ((), ()))
NY, NZ, NO = 4, 16, 8
SUBS = 4


def mm(a, b, dims=NN):
    return lax.dot_general(a, b, dims, preferred_element_type=F32)


def exchange_kernel(slot_ref, ch_ref, out_ref, stage, send_sem, recv_sem):
    leaf, octant = lax.axis_index("leaf"), lax.axis_index("oct")
    barrier = pltpu.get_barrier_semaphore()
    for d in range(1, NO):
        pl.semaphore_signal(
            barrier, inc=1, device_id=(leaf, lax.rem(octant + d, NO)), device_id_type=MESH
        )
    for q in range(32):
        stage[q // 4, q % 4] = ch_ref[slot_ref[q]]
    pl.semaphore_wait(barrier, NO - 1)
    copies = []
    for d in range(1, NO):
        target = lax.rem(octant + d, NO)
        copy = pltpu.make_async_remote_copy(
            src_ref=stage.at[target],
            dst_ref=out_ref.at[octant],
            send_sem=send_sem.at[d],
            recv_sem=recv_sem.at[d],
            device_id=(leaf, target),
            device_id_type=MESH,
        )
        copy.start()
        copies.append(copy)
    out_ref[octant] = stage[octant]
    for copy in copies:
        copy.wait()


def exchange(slots, child_cubes):
    return pl.pallas_call(
        exchange_kernel,
        out_shape=jax.ShapeDtypeStruct((NO, 4, 16, 256), BF),
        in_specs=[pl.BlockSpec(memory_space=pltpu.SMEM), VM],
        out_specs=VM,
        scratch_shapes=[
            pltpu.VMEM((NO, 4, 16, 256), BF),
            pltpu.SemaphoreType.DMA((NO,)),
            pltpu.SemaphoreType.DMA((NO,)),
        ],
        compiler_params=pltpu.CompilerParams(collective_id=0, has_side_effects=True),
        name="exchange",
    )(slots, child_cubes)


def apply_kernel(
    b_ref, f_ref, w_ref, wt_ref, wtd_ref, wc4_ref, bd_ref, out_ref,
    mask2, mask3, s1, base2, base3, lhs3, e3, totals,
):
    row = lax.broadcasted_iota(jnp.int32, (256, 256), 0)
    col = lax.broadcasted_iota(jnp.int32, (256, 256), 1)
    mask2[...] = jnp.where(col % 8 == (row // 16) % 8, 1.0, 0.0).astype(BF)
    mask3[...] = jnp.where(col % 8 == (row // 8) % 8, 1.0, 0.0).astype(BF)

    def entry(n, carry):
        p = n // 4
        x_rows = []
        for i in range(2):
            tiles = []
            for j in range(2):
                for vh in range(2):
                    for l in range(2):
                        tiles.append(b_ref[4 * i + 2 * j + l, p, :, vh * 128:(vh + 1) * 128])
            x_rows.append(jnp.concatenate(tiles, axis=1))
        x = jnp.concatenate(x_rows, axis=0)
        g0 = mm(f_ref[n, 0:320, :], w_ref[...]).astype(BF)
        h0 = mm(bd_ref[...], g0).astype(BF)
        s1[...] = mm(h0, x).astype(BF)
        a1 = mm(wtd_ref[...], f_ref[n, 320:640, :], NT).astype(BF)
        a2 = mm(wt_ref[...], f_ref[n, 640:960, :], NT).astype(BF)
        for g, width in ((0, 128), (1, 128), (2, 64)):
            ins = slice(g * 128, g * 128 + width)
            outs = slice(g * 1024, g * 1024 + width * 8)
            base3[:, outs] = mm(a1[:, ins], wc4_ref[0:width, 0:width * 8]).astype(BF)
            base2[:, outs] = mm(a2[:, ins], wc4_ref[0:width, 0:width * 8]).astype(BF)
        for t in range(10):
            lanes = slice(t * 256, (t + 1) * 256)
            for bh in range(4):
                for cp in range(4):
                    r = bh * 64 + cp * 16
                    e3[t * 256 + r:t * 256 + r + 16, :] = (
                        base3[bh * 16:(bh + 1) * 16, lanes] * mask3[r:r + 16, :]
                    )
            e2 = jnp.concatenate(
                [base2[0:16, lanes]] * 8 + [base2[16:32, lanes]] * 8, axis=0
            ) * mask2[...]
            lhs2 = jnp.concatenate(
                [s1[t * 32:(t + 1) * 32, bh * 256:(bh + 1) * 256] for bh in range(4)], axis=0
            )
            mid = mm(lhs2, e2)
            for ch in range(4):
                lhs3[ch * 32:(ch + 1) * 32, lanes] = jnp.concatenate(
                    [mid[bh * 32:(bh + 1) * 32, ch * 64:(ch + 1) * 64] for bh in range(4)], axis=1
                ).astype(BF)
        total = mm(lhs3[...], e3[...])
        for i in range(2):
            for j in range(2):
                for l in range(2):
                    for wh in range(2):
                        r = (2 * l + wh) * 32 + i * 16
                        start = pl.multiple_of(n * 32 + wh * 16, 16)
                        totals[4 * i + 2 * j + l, pl.ds(start, 16), :] = total[
                            r:r + 16, j * 128:(j + 1) * 128
                        ]
        return carry

    lax.fori_loop(0, 16, entry, 0)

    def spread(o, carry):
        for r in range(32):
            out_ref[o, r] = totals[o, pl.ds(r, 16, stride=32), :].astype(BF)
        return carry

    lax.fori_loop(0, NO, spread, 0)


def apply_entries(blocks, kind_factors, two_scale):
    wt = two_scale.T
    wtd = jnp.broadcast_to(wt.reshape(4, 1, 8, 32), (4, 2, 8, 32)).reshape(64, 32)
    wc = jnp.repeat(two_scale, 8, axis=1)
    wc4 = jnp.kron(jnp.eye(4, dtype=BF), wc)
    bd = jnp.kron(jnp.eye(10, dtype=BF), wt)
    return pl.pallas_call(
        apply_kernel,
        out_shape=jax.ShapeDtypeStruct((NO, 32, 16, 128), BF),
        in_specs=[VM] * 7,
        out_specs=VM,
        scratch_shapes=[
            pltpu.VMEM((256, 256), BF),
            pltpu.VMEM((256, 256), BF),
            pltpu.VMEM((320, 1024), BF),
            pltpu.VMEM((32, 2560), BF),
            pltpu.VMEM((64, 2560), BF),
            pltpu.VMEM((128, 2560), BF),
            pltpu.VMEM((2560, 256), BF),
            pltpu.VMEM((NO, 512, 128), F32),
        ],
        compiler_params=pltpu.CompilerParams(vmem_limit_bytes=48 << 20),
        name="apply_entries",
    )(blocks, kind_factors, two_scale, wt, wtd, wc4, bd)


def deliver_kernel(
    c_ref, id_ref, out_ref, rows, idx, idy, part, from_low, from_high,
    xs, xr, ixs, ixr, ys, yr, fs, fr, iys, iyr, ps, pr, ms, mr,
):
    leaf, octant = lax.axis_index("leaf"), lax.axis_index("oct")
    z, y = leaf // NY, lax.rem(leaf, NY)

    def at_y(d):
        return (z * NY + lax.rem(y + d, NY), octant)

    up_z = (lax.rem(z + 1, NZ) * NY + y, octant)
    down_z = (lax.rem(z + NZ - 1, NZ) * NY + y, octant)

    def remote(src, dst, ss, rs, where):
        copy = pltpu.make_async_remote_copy(
            src_ref=src, dst_ref=dst, send_sem=ss, recv_sem=rs, device_id=where,
            device_id_type=MESH,
        )
        copy.start()
        return copy

    barrier = pltpu.get_barrier_semaphore()
    partners = [(leaf, lax.rem(octant + d, NO)) for d in range(1, NO)]
    partners += [at_y(1), at_y(2), at_y(3), up_z, down_z]
    for partner in partners:
        pl.semaphore_signal(barrier, inc=1, device_id=partner, device_id_type=MESH)
    pl.semaphore_wait(barrier, len(partners))

    x_copies, ix_copies = [], []
    for d in range(1, NO):
        target = lax.rem(octant + d, NO)
        where = (leaf, target)
        ix_copies.append(remote(id_ref, idx.at[octant], ixs.at[d], ixr.at[d], where))
        x_copies.append(
            remote(c_ref.at[target], rows.at[y, octant], xs.at[d], xr.at[d], where)
        )
    rows[y, octant] = c_ref[octant]
    idx[octant] = id_ref[...]

    y_copies = []

    def send_y(d):
        source = lax.rem(octant + NO - d, NO)
        block = rows.at[y, source]
        y_copies.append((
            remote(block, block, ys.at[0, d], yr.at[0, d], at_y(1)),
            remote(block, block, ys.at[1, d], yr.at[1, d], at_y(3)),
        ))

    send_y(0)
    for copy in ix_copies:
        copy.wait()
    idy[y] = jnp.sum(idx[...], axis=0)
    iy_copies = [
        remote(idy.at[y], idy.at[y], iys.at[d], iyr.at[d], at_y(d)) for d in range(1, NY)
    ]
    f_copies = []

    def forward(d):
        source = lax.rem(octant + NO - d, NO)
        up, down = y_copies[d]
        up.wait_recv()
        down.wait_recv()
        if d < 4:
            block = rows.at[lax.rem(y + NY - 1, NY), source]
            f_copies.append(remote(block, block, fs.at[d], fr.at[d], at_y(1)))
        else:
            block = rows.at[lax.rem(y + 1, NY), source]
            f_copies.append(remote(block, block, fs.at[d], fr.at[d], at_y(3)))

    for d in range(1, NO):
        x_copies[d - 1].wait()
        send_y(d)
    for d in range(NO):
        forward(d)
    for copy in iy_copies:
        copy.wait()
    for copy in f_copies:
        copy.wait()
    for up, down in y_copies:
        up.wait_send()
        down.wait_send()

    rho = lax.broadcasted_iota(jnp.int32, (256, 128), 0)
    key = (rho // 16) * 64 + y * 16 + rho % 16
    select = jnp.concatenate(
        [jnp.where(key == idy[s][0:1, :], 1.0, 0.0).astype(BF) for s in range(NY)], axis=1
    )

    def node_sums(r, carry):
        lo = rows[:, :, 2 * r].reshape(512, 128)
        hi = rows[:, :, 2 * r + 1].reshape(512, 128)
        sums = mm(select, jnp.concatenate([lo, hi], axis=1)).astype(BF)
        part[:, 2 * r] = sums[:, 0:128].reshape(NZ, 16, 128)
        part[:, 2 * r + 1] = sums[:, 128:256].reshape(NZ, 16, 128)
        return carry

    lax.fori_loop(0, 16, node_sums, 0)

    width = 32 // SUBS
    up_copies, down_copies = {}, {}
    for s in range(8):
        high = lax.rem(z + 8 - s, NZ)
        low = lax.rem(z + NZ - 7 + s, NZ)
        for u in range(SUBS):
            span = pl.ds(u * width, width)
            if s > 0:
                up_copies[s - 1, u].wait_recv()
                part[high, span] = part[high, span] + from_low[s - 1, span]
            up_copies[s, u] = remote(
                part.at[high, span], from_low.at[s, span], ps.at[s, u], pr.at[s, u], up_z
            )
            if s < 7:
                if s > 0:
                    down_copies[s - 1, u].wait_recv()
                    part[low, span] = part[low, span] + from_high[s - 1, span]
                down_copies[s, u] = remote(
                    part.at[low, span], from_high.at[s, span], ms.at[s, u], mr.at[s, u], down_z
                )
    row = lax.broadcasted_iota(jnp.int32, (256, 256), 0)
    col = lax.broadcasted_iota(jnp.int32, (256, 256), 1)
    source_lane = (col % 16) // 8 * 128 + (col // 16) * 8 + col % 8
    perm = jnp.where(row == source_lane, 1.0, 0.0).astype(BF)
    for u in range(SUBS):
        down_copies[6, u].wait_recv()
        up_copies[7, u].wait_recv()
    for u in range(16):
        pieces = []
        for wh in range(2):
            r = wh * 16 + u
            pieces.append((
                part[z, r].astype(F32) + from_low[7, r].astype(F32) + from_high[6, r].astype(F32)
            ).astype(BF))
        out_ref[:, u * 256:(u + 1) * 256] = mm(
            jnp.concatenate(pieces, axis=1), perm
        ).astype(BF)
    for copy in list(up_copies.values()) + list(down_copies.values()):
        copy.wait_send()


def deliver(pieces, ids):
    dma = pltpu.SemaphoreType.DMA
    return pl.pallas_call(
        deliver_kernel,
        out_shape=jax.ShapeDtypeStruct((16, 4096), BF),
        in_specs=[VM, VM],
        out_specs=VM,
        scratch_shapes=[
            pltpu.VMEM((NY, NO, 32, 16, 128), BF),
            pltpu.VMEM((NO, 8, 128), jnp.int32),
            pltpu.VMEM((NY, 8, 128), jnp.int32),
            pltpu.VMEM((NZ, 32, 16, 128), BF),
            pltpu.VMEM((8, 32, 16, 128), BF),
            pltpu.VMEM((7, 32, 16, 128), BF),
            dma((NO,)), dma((NO,)), dma((NO,)), dma((NO,)),
            dma((2, NO)), dma((2, NO)), dma((NO,)), dma((NO,)), dma((NY,)), dma((NY,)),
            dma((8, SUBS)), dma((8, SUBS)), dma((7, SUBS)), dma((7, SUBS)),
        ],
        compiler_params=pltpu.CompilerParams(
            collective_id=1, has_side_effects=True, vmem_limit_bytes=48 << 20
        ),
        name="deliver",
    )(pieces, ids)


def local(children, child_slot, two_scale, factors, disp_kind, target_leaf, target_node):
    kind_factors = factors[disp_kind.reshape(-1)].reshape(16, 960, 32)
    blocks = exchange(child_slot.reshape(-1), children.reshape(32, 16, 256))
    pieces = apply_entries(blocks, kind_factors, two_scale)
    goal = target_leaf.reshape(-1) * 16 + target_node.reshape(-1)
    lane = jnp.arange(128, dtype=jnp.int32)
    ids = jnp.where(lane // 16 == lax.axis_index("oct"), jnp.tile(goal, 8), 0)
    ids = jnp.broadcast_to(ids[None, :], (8, 128))
    return deliver(pieces, ids).reshape(16, 1, 4096)


def solution(mesh):
    placed = (
        P(("leaf", "oct"), None),
        P("leaf", "oct"),
        P(),
        P(),
        P(("leaf", "oct"), None),
        P(("leaf", "oct"), None, None),
        P(("leaf", "oct"), None),
    )
    return jax.shard_map(
        local, mesh=mesh, in_specs=placed, out_specs=P("leaf", "oct", None), check_vma=False
    )
```

```python
import functools

import jax
import jax.numpy as jnp
from jax import lax
from jax.experimental import pallas as pl
from jax.experimental.pallas import tpu as pltpu
from jax.sharding import PartitionSpec as P

BF = jnp.bfloat16
F32 = jnp.float32
MESH = pl.DeviceIdType.MESH
VM = pl.BlockSpec(memory_space=pltpu.VMEM)
NT = (((1,), (1,)), ((), ()))
NN = (((1,), (0,)), ((), ()))
NY, NZ, NO = 4, 16, 8
SUBS = 4
NP = 4


def mm(a, b, dims=NN):
    return lax.dot_general(a, b, dims, preferred_element_type=F32)


def apply_all_kernel(
    slot_ref, kind_ref, ch_ref, tab_ref, w_ref, wt_ref, wtd_ref, wc4_ref, bd_ref, id_ref, out_ref,
    stage, blocks, mask2, mask3, flat, h0s, base2, base3, s1, lhs3, e3, totals, pieces,
    rows, idx, idy, select, acc, part, from_low, from_high,
    es, er, xs, xr, ixs, ixr, ys, yr, fs, fr, iys, iyr, ps, pr, ms, mr,
):
    leaf, octant = lax.axis_index("leaf"), lax.axis_index("oct")
    z, y = leaf // NY, lax.rem(leaf, NY)

    def at_y(d):
        return (z * NY + lax.rem(y + d, NY), octant)

    up_z = (lax.rem(z + 1, NZ) * NY + y, octant)
    down_z = (lax.rem(z + NZ - 1, NZ) * NY + y, octant)
    targets = [lax.rem(octant + d, NO) for d in range(NO)]

    def remote(src, dst, ss, rs, where):
        copy = pltpu.make_async_remote_copy(
            src_ref=src, dst_ref=dst, send_sem=ss, recv_sem=rs, device_id=where,
            device_id_type=MESH,
        )
        copy.start()
        return copy

    barrier = pltpu.get_barrier_semaphore()
    partners = [(leaf, targets[d]) for d in range(1, NO)]
    partners += [at_y(1), at_y(2), at_y(3), up_z, down_z]
    for partner in partners:
        pl.semaphore_signal(barrier, inc=1, device_id=partner, device_id_type=MESH)
    for q in range(32):
        stage[q // 4, q % 4] = ch_ref[slot_ref[q]]
    idx[octant] = id_ref[...]
    pl.semaphore_wait(barrier, len(partners))

    e_copies, ix_copies = [], []
    for d in range(1, NO):
        where = (leaf, targets[d])
        e_copies.append(
            remote(stage.at[targets[d]], blocks.at[octant], es.at[d], er.at[d], where)
        )
    for d in range(1, NO):
        where = (leaf, targets[d])
        ix_copies.append(remote(id_ref, idx.at[octant], ixs.at[d], ixr.at[d], where))
    blocks[octant] = stage[octant]

    row = lax.broadcasted_iota(jnp.int32, (256, 256), 0)
    col = lax.broadcasted_iota(jnp.int32, (256, 256), 1)
    mask2[...] = jnp.where(col % 8 == (row // 16) % 8, 1.0, 0.0).astype(BF)
    mask3[...] = jnp.where(col % 8 == (row // 8) % 8, 1.0, 0.0).astype(BF)

    def fold(n, carry):
        dense = tab_ref[kind_ref[n]].astype(F32)
        for o in range(4):
            flat[pl.ds(o, 240, stride=4), :] = dense[:, o * 32:(o + 1) * 32]
        g0 = mm(flat[0:320, :].astype(BF), w_ref[...]).astype(BF)
        h0s[n] = mm(bd_ref[...], g0).astype(BF)
        a1 = mm(wtd_ref[...], flat[320:640, :].astype(BF), NT).astype(BF)
        a2 = mm(wt_ref[...], flat[640:960, :].astype(BF), NT).astype(BF)
        for g, width in ((0, 128), (1, 128), (2, 64)):
            ins = slice(g * 128, g * 128 + width)
            outs = slice(g * 1024, g * 1024 + width * 8)
            base3[n, :, outs] = mm(a1[:, ins], wc4_ref[0:width, 0:width * 8]).astype(BF)
            base2[n, :, outs] = mm(a2[:, ins], wc4_ref[0:width, 0:width * 8]).astype(BF)
        return carry

    lax.fori_loop(0, 16, fold, 0)
    for copy in e_copies:
        copy.wait()

    x_copies, y_copies, f_copies = {}, {}, {}

    def send_x(p):
        for d in range(1, NO):
            x_copies[p, d] = remote(
                pieces.at[p, targets[d]], rows.at[y, p, octant], xs.at[p, d], xr.at[p, d],
                (leaf, targets[d]),
            )
        rows[y, p, octant] = pieces[p, octant]

    def send_y(p):
        for d in range(1, NO):
            x_copies[p, d].wait_recv()
        block = rows.at[y, p]
        y_copies[p] = (
            remote(block, block, ys.at[0, p], yr.at[0, p], at_y(1)),
            remote(block, block, ys.at[1, p], yr.at[1, p], at_y(3)),
        )

    def forward(p):
        up, down = y_copies[p]
        up.wait_recv()
        block = rows.at[lax.rem(y + NY - 1, NY), p, 0:4]
        first = remote(block, block, fs.at[0, p], fr.at[0, p], at_y(1))
        down.wait_recv()
        block = rows.at[lax.rem(y + 1, NY), p, 4:8]
        second = remote(block, block, fs.at[1, p], fr.at[1, p], at_y(3))
        f_copies[p] = (first, second)

    iy_copies = []
    for p in range(NP):
        x_rows = []
        for i in range(2):
            tiles = []
            for j in range(2):
                for vh in range(2):
                    for l in range(2):
                        tiles.append(blocks[4 * i + 2 * j + l, p, :, vh * 128:(vh + 1) * 128])
            x_rows.append(jnp.concatenate(tiles, axis=1))
        x = jnp.concatenate(x_rows, axis=0)

        def entry(k, carry):
            n = p * 4 + k
            s1[...] = mm(h0s[n], x).astype(BF)
            for t in range(10):
                lanes = slice(t * 256, (t + 1) * 256)
                for bh in range(4):
                    tile = base3[n, bh * 16:(bh + 1) * 16, lanes]
                    for cp in range(4):
                        r = bh * 64 + cp * 16
                        e3[t * 256 + r:t * 256 + r + 16, :] = tile * mask3[r:r + 16, :]
                low, high = base2[n, 0:16, lanes], base2[n, 16:32, lanes]
                e2 = jnp.concatenate([low] * 8 + [high] * 8, axis=0) * mask2[...]
                lhs2 = jnp.concatenate(
                    [s1[t * 32:(t + 1) * 32, bh * 256:(bh + 1) * 256] for bh in range(4)], axis=0
                )
                mid = mm(lhs2, e2)
                for ch in range(4):
                    lhs3[ch * 32:(ch + 1) * 32, lanes] = jnp.concatenate(
                        [mid[bh * 32:(bh + 1) * 32, ch * 64:(ch + 1) * 64] for bh in range(4)],
                        axis=1,
                    ).astype(BF)
            total = mm(lhs3[...], e3[...])
            for i in range(2):
                for j in range(2):
                    for l in range(2):
                        for wh in range(2):
                            r = (2 * l + wh) * 32 + i * 16
                            start = pl.multiple_of(k * 32 + wh * 16, 16)
                            totals[4 * i + 2 * j + l, pl.ds(start, 16), :] = total[
                                r:r + 16, j * 128:(j + 1) * 128
                            ]
            return carry

        lax.fori_loop(0, 3, entry, 0)
        if p == 0:
            for copy in ix_copies:
                copy.wait()
            idy[y] = jnp.sum(idx[...], axis=0)
            for d in range(1, NY):
                iy_copies.append(remote(idy.at[y], idy.at[y], iys.at[d], iyr.at[d], at_y(d)))
        if p >= 1:
            send_y(p - 1)
        lax.fori_loop(3, 4, entry, 0)
        for o in range(NO):
            for r in range(8):
                pieces[p, o, r] = totals[o, pl.ds(r, 16, stride=8), :].astype(BF)
        send_x(p)
        if p >= 2:
            forward(p - 2)

    rho = lax.broadcasted_iota(jnp.int32, (256, 128), 0)
    key = (rho // 16) * 64 + y * 16 + rho % 16
    lane = lax.broadcasted_iota(jnp.int32, (256, 128), 1)

    def node_sums(p):
        for h in range(4):
            for s in range(NY):
                hit = (key == idy[s, p:p + 1, :]) & (lane % 4 == h)
                select[h, :, s * 128:(s + 1) * 128] = jnp.where(hit, 1.0, 0.0).astype(BF)
        for copy in f_copies[p]:
            copy.wait_recv()

        def two_rows(r, carry):
            lo = rows[:, p, :, 2 * r].reshape(512, 128)
            hi = rows[:, p, :, 2 * r + 1].reshape(512, 128)
            both = jnp.concatenate([lo, hi], axis=1)
            for h in range(4):
                new = mm(select[h], both)
                if p > 0:
                    new = new + acc[h, r]
                if p < NP - 1:
                    acc[h, r] = new
                else:
                    new = new.astype(BF)
                    part[:, h * 8 + 2 * r] = new[:, 0:128].reshape(NZ, 16, 128)
                    part[:, h * 8 + 2 * r + 1] = new[:, 128:256].reshape(NZ, 16, 128)
            return carry

        lax.fori_loop(0, 4, two_rows, 0)

    for copy in iy_copies:
        copy.wait()
    node_sums(0)
    send_y(3)
    forward(2)
    node_sums(1)
    forward(3)
    node_sums(2)
    node_sums(3)

    width = 32 // SUBS
    up_copies, down_copies = {}, {}
    for s in range(8):
        high = lax.rem(z + 8 - s, NZ)
        low = lax.rem(z + NZ - 7 + s, NZ)
        for u in range(SUBS):
            span = pl.ds(u * width, width)
            if s > 0:
                up_copies[s - 1, u].wait_recv()
                part[high, span] = part[high, span] + from_low[s - 1, span]
            up_copies[s, u] = remote(
                part.at[high, span], from_low.at[s, span], ps.at[s, u], pr.at[s, u], up_z
            )
            if s < 7:
                if s > 0:
                    down_copies[s - 1, u].wait_recv()
                    part[low, span] = part[low, span] + from_high[s - 1, span]
                down_copies[s, u] = remote(
                    part.at[low, span], from_high.at[s, span], ms.at[s, u], mr.at[s, u], down_z
                )
    row = lax.broadcasted_iota(jnp.int32, (256, 256), 0)
    col = lax.broadcasted_iota(jnp.int32, (256, 256), 1)
    source_lane = (col % 16) // 8 * 128 + (col // 16) * 8 + col % 8
    perm = jnp.where(row == source_lane, 1.0, 0.0).astype(BF)
    for u in range(SUBS):
        down_copies[6, u].wait_recv()
        up_copies[7, u].wait_recv()
    for u in range(16):
        pair = []
        for wh in range(2):
            r = wh * 16 + u
            pair.append((
                part[z, r].astype(F32) + from_low[7, r].astype(F32) + from_high[6, r].astype(F32)
            ).astype(BF))
        out_ref[:, u * 256:(u + 1) * 256] = mm(
            jnp.concatenate(pair, axis=1), perm
        ).astype(BF)
    for copy in list(up_copies.values()) + list(down_copies.values()):
        copy.wait_send()
    for p in range(NP):
        for copy in f_copies[p] + y_copies[p]:
            copy.wait_send()
        for d in range(1, NO):
            x_copies[p, d].wait_send()


def apply_all(slots, kinds, child_cubes, table, two_scale, ids):
    dma = pltpu.SemaphoreType.DMA
    smem = pl.BlockSpec(memory_space=pltpu.SMEM)
    wt = two_scale.T
    wtd = jnp.broadcast_to(wt.reshape(4, 1, 8, 32), (4, 2, 8, 32)).reshape(64, 32)
    wc4 = jnp.kron(jnp.eye(4, dtype=BF), jnp.repeat(two_scale, 8, axis=1))
    bd = jnp.kron(jnp.eye(10, dtype=BF), wt)
    return pl.pallas_call(
        apply_all_kernel,
        out_shape=jax.ShapeDtypeStruct((16, 4096), BF),
        in_specs=[smem, smem] + [VM] * 8,
        out_specs=VM,
        scratch_shapes=[
            pltpu.VMEM((NO, NP, 16, 256), BF),
            pltpu.VMEM((NO, NP, 16, 256), BF),
            pltpu.VMEM((256, 256), BF),
            pltpu.VMEM((256, 256), BF),
            pltpu.VMEM((960, 32), F32),
            pltpu.VMEM((16, 320, 32), BF),
            pltpu.VMEM((16, 32, 2560), BF),
            pltpu.VMEM((16, 64, 2560), BF),
            pltpu.VMEM((320, 1024), BF),
            pltpu.VMEM((128, 2560), BF),
            pltpu.VMEM((2560, 256), BF),
            pltpu.VMEM((NO, 128, 128), F32),
            pltpu.VMEM((NP, NO, 8, 16, 128), BF),
            pltpu.VMEM((NY, NP, NO, 8, 16, 128), BF),
            pltpu.VMEM((NO, 8, 128), jnp.int32),
            pltpu.VMEM((NY, 8, 128), jnp.int32),
            pltpu.VMEM((4, 256, 512), BF),
            pltpu.VMEM((4, 4, 256, 256), F32),
            pltpu.VMEM((NZ, 32, 16, 128), BF),
            pltpu.VMEM((8, 32, 16, 128), BF),
            pltpu.VMEM((7, 32, 16, 128), BF),
            dma((NO,)), dma((NO,)), dma((NP, NO)), dma((NP, NO)), dma((NO,)), dma((NO,)),
            dma((2, NP)), dma((2, NP)), dma((2, NP)), dma((2, NP)), dma((NY,)), dma((NY,)),
            dma((8, SUBS)), dma((8, SUBS)), dma((7, SUBS)), dma((7, SUBS)),
        ],
        compiler_params=pltpu.CompilerParams(
            collective_id=0, has_side_effects=True, vmem_limit_bytes=56 << 20
        ),
        name="apply_all",
    )(slots, kinds, child_cubes, table, two_scale, wt, wtd, wc4, bd, ids)


def local(children, child_slot, two_scale, factors, disp_kind, target_leaf, target_node):
    goal = (target_leaf[:, :, 0] * 16 + target_node).astype(jnp.int32)
    lane = jnp.arange(128, dtype=jnp.int32)
    spread = jnp.tile(jnp.repeat(goal, 4, axis=1), (1, NO))
    ids = jnp.where(lane // 16 == lax.axis_index("oct"), spread, 0)
    out = apply_all(
        child_slot.reshape(-1), disp_kind.reshape(-1), children.reshape(32, 16, 256),
        factors.reshape(-1, 240, 128), two_scale, jnp.pad(ids, ((0, 4), (0, 0))),
    )
    return out.reshape(16, 1, 4096)


def solution(mesh):
    placed = (
        P(("leaf", "oct"), None),
        P("leaf", "oct"),
        P(),
        P(),
        P(("leaf", "oct"), None),
        P(("leaf", "oct"), None, None),
        P(("leaf", "oct"), None),
    )
    return jax.shard_map(
        local, mesh=mesh, in_specs=placed, out_specs=P("leaf", "oct", None), check_vma=False
    )
```

```python
import functools

import jax
import jax.numpy as jnp
from jax import lax
from jax.experimental import pallas as pl
from jax.experimental.pallas import tpu as pltpu
from jax.sharding import PartitionSpec as P

BF = jnp.bfloat16
F32 = jnp.float32
MESH = pl.DeviceIdType.MESH
VM = pl.BlockSpec(memory_space=pltpu.VMEM)
NT = (((1,), (1,)), ((), ()))
NN = (((1,), (0,)), ((), ()))
NY, NZ, NO = 4, 16, 8
SUBS = 4
NP = 4


def mm(a, b, dims=NN):
    return lax.dot_general(a, b, dims, preferred_element_type=F32)


def one_hot(hit):
    return jnp.where(hit, 1.0, 0.0).astype(BF)


def iotas(rows, cols):
    return (
        lax.broadcasted_iota(jnp.int32, (rows, cols), 0),
        lax.broadcasted_iota(jnp.int32, (rows, cols), 1),
    )


def apply_all_kernel(
    slot_ref, kind_ref, leaf_ref, node_ref, ch_ref, tab_ref, w_ref, out_ref,
    stage, blocks, mask2, mask3, wt, wtd, wc4, bd, flat, h0s, base2, base3, s1, lhs3, e3,
    totals, pieces, rows, idx, idy, select, acc, part, from_low, from_high,
    es, er, xs, xr, ixs, ixr, ys, yr, fs, fr, iys, iyr, ps, pr, ms, mr,
):
    leaf, octant = lax.axis_index("leaf"), lax.axis_index("oct")
    z, y = leaf // NY, lax.rem(leaf, NY)
    chip, core = octant // 2, lax.rem(octant, 2)

    def at_y(d):
        return (z * NY + lax.rem(y + d, NY), octant)

    up_z = (lax.rem(z + 1, NZ) * NY + y, octant)
    down_z = (lax.rem(z + NZ - 1, NZ) * NY + y, octant)
    hops = [(2, 0), (2, 1), (1, 0), (1, 1), (3, 0), (3, 1), (0, 1)]
    target = {(e, c): lax.rem(chip + e, 4) * 2 + lax.rem(core + c, 2) for e, c in hops}

    def remote(src, dst, ss, rs, where):
        copy = pltpu.make_async_remote_copy(
            src_ref=src, dst_ref=dst, send_sem=ss, recv_sem=rs, device_id=where,
            device_id_type=MESH,
        )
        copy.start()
        return copy

    barrier = pltpu.get_barrier_semaphore()
    partners = [(leaf, target[hop]) for hop in hops]
    partners += [at_y(1), at_y(2), at_y(3), up_z, down_z]
    for partner in partners:
        pl.semaphore_signal(barrier, inc=1, device_id=partner, device_id_type=MESH)
    for q in range(32):
        stage[q // 4, q % 4] = ch_ref[slot_ref[q, 0]]
    row, col = iotas(8, 128)
    goal = jnp.zeros((8, 128), jnp.int32)
    for p in range(NP):
        for k in range(4):
            goal = jnp.where(
                (row == p) & (col % 16 // 4 == k), leaf_ref[p, k] * 16 + node_ref[p, k], goal
            )
    idx[octant] = jnp.where(col // 16 == octant, goal, 0)
    pl.semaphore_wait(barrier, len(partners))

    e_copies, ix_copies = [], []
    for e, c in hops:
        to = target[e, c]
        e_copies.append(
            remote(stage.at[to], blocks.at[octant], es.at[e, c], er.at[e, c], (leaf, to))
        )
    for e, c in hops:
        to = target[e, c]
        ix_copies.append(
            remote(idx.at[octant], idx.at[octant], ixs.at[e, c], ixr.at[e, c], (leaf, to))
        )
    blocks[octant] = stage[octant]

    w = w_ref[...]
    row, col = iotas(256, 256)
    mask2[...] = one_hot(col % 8 == (row // 16) % 8)
    mask3[...] = one_hot(col % 8 == (row // 8) % 8)
    row, col = iotas(32, 32)
    wt[...] = mm(one_hot(row == col), w, NT).astype(BF)
    row, col = iotas(64, 32)
    wtd[...] = mm(one_hot(col == row // 16 * 8 + row % 8), w, NT).astype(BF)
    row, col = iotas(320, 32)
    tile = one_hot(row % 32 == col)
    row, col = iotas(32, 1024)
    wide = mm(w, one_hot(col % 256 // 8 == row)).astype(BF)
    row, col = iotas(128, 1024)
    wc4[...] = jnp.where(row // 32 == col // 256, mm(tile[0:128], wide), 0.0).astype(BF)
    row, col = iotas(320, 320)
    tall = mm(tile, w, NT).astype(BF)
    bd[...] = jnp.where(row // 32 == col // 32, mm(tall, tile, NT), 0.0).astype(BF)

    def fold(p, k):
        n = p * 4 + k
        dense = tab_ref[kind_ref[p, k]].astype(F32)
        for o in range(4):
            flat[pl.ds(o, 240, stride=4), :] = dense[:, o * 32:(o + 1) * 32]
        g0 = mm(flat[0:320, :].astype(BF), w_ref[...]).astype(BF)
        h0s[n] = mm(bd[...], g0).astype(BF)
        a1 = mm(wtd[...], flat[320:640, :].astype(BF), NT).astype(BF)
        a2 = mm(wt[...], flat[640:960, :].astype(BF), NT).astype(BF)
        for g, width in ((0, 128), (1, 128), (2, 64)):
            ins = slice(g * 128, g * 128 + width)
            outs = slice(g * 1024, g * 1024 + width * 8)
            base3[n, :, outs] = mm(a1[:, ins], wc4[0:width, 0:width * 8]).astype(BF)
            base2[n, :, outs] = mm(a2[:, ins], wc4[0:width, 0:width * 8]).astype(BF)

    def fold_first(k, carry):
        fold(0, k)
        return carry

    lax.fori_loop(0, 4, fold_first, 0)
    for copy in e_copies:
        copy.wait()

    x_copies, y_copies, f_copies = {}, {}, {}

    def send_x(p):
        rows[y, p, octant] = pieces[p, octant]
        for e, c in hops:
            to = target[e, c]
            x_copies[p, e, c] = remote(
                pieces.at[p, to], rows.at[y, p, octant], xs.at[p, e, c], xr.at[p, e, c],
                (leaf, to),
            )

    def pair_of(e):
        return pl.ds(lax.rem(chip + 4 - e, 4) * 2, 2)

    def send_y(p, e):
        for c in range(2):
            if (e, c) != (0, 0):
                x_copies[p, e, c].wait_recv()
        block = rows.at[y, p, pair_of(e)]
        y_copies[p, e] = (
            remote(block, block, ys.at[0, p, e], yr.at[0, p, e], at_y(1)),
            remote(block, block, ys.at[1, p, e], yr.at[1, p, e], at_y(3)),
        )

    def forward(p, *which):
        for e in which:
            up, down = y_copies[p, e]
            up.wait_recv()
            down.wait_recv()
            came, to = (NY - 1, 1) if e < 2 else (1, 3)
            block = rows.at[lax.rem(y + came, NY), p, pair_of(e)]
            f_copies[p, e] = remote(block, block, fs.at[p, e], fr.at[p, e], at_y(to))

    iy_copies = []
    for p in range(NP):
        x_rows = []
        for i in range(2):
            tiles = []
            for j in range(2):
                for vh in range(2):
                    for l in range(2):
                        tiles.append(blocks[4 * i + 2 * j + l, p, :, vh * 128:(vh + 1) * 128])
            x_rows.append(jnp.concatenate(tiles, axis=1))
        x = jnp.concatenate(x_rows, axis=0)

        def entry(k, carry):
            n = p * 4 + k
            s1[...] = mm(h0s[n], x).astype(BF)
            for t in range(10):
                lanes = slice(t * 256, (t + 1) * 256)
                for bh in range(4):
                    tile = base3[n, bh * 16:(bh + 1) * 16, lanes]
                    for cp in range(4):
                        r = bh * 64 + cp * 16
                        e3[t * 256 + r:t * 256 + r + 16, :] = tile * mask3[r:r + 16, :]
                low, high = base2[n, 0:16, lanes], base2[n, 16:32, lanes]
                e2 = jnp.concatenate([low] * 8 + [high] * 8, axis=0) * mask2[...]
                lhs2 = jnp.concatenate(
                    [s1[t * 32:(t + 1) * 32, bh * 256:(bh + 1) * 256] for bh in range(4)], axis=0
                )
                mid = mm(lhs2, e2)
                for ch in range(4):
                    lhs3[ch * 32:(ch + 1) * 32, lanes] = jnp.concatenate(
                        [mid[bh * 32:(bh + 1) * 32, ch * 64:(ch + 1) * 64] for bh in range(4)],
                        axis=1,
                    ).astype(BF)
            total = mm(lhs3[...], e3[...])
            for i in range(2):
                for j in range(2):
                    for l in range(2):
                        for wh in range(2):
                            r = (2 * l + wh) * 32 + i * 16
                            start = pl.multiple_of(k * 32 + wh * 16, 16)
                            totals[4 * i + 2 * j + l, pl.ds(start, 16), :] = total[
                                r:r + 16, j * 128:(j + 1) * 128
                            ]
            if p < NP - 1:
                fold(p + 1, k)
            return carry

        lax.fori_loop(0, 2, entry, 0)
        if p == 0:
            for copy in ix_copies:
                copy.wait()
            idy[y] = jnp.sum(idx[...], axis=0)
            for d in range(1, NY):
                iy_copies.append(remote(idy.at[y], idy.at[y], iys.at[d], iyr.at[d], at_y(d)))
        else:
            send_y(p - 1, 0)
        if p >= 2:
            send_y(p - 2, 2)
        if p >= 3:
            forward(p - 3, 2)
        lax.fori_loop(2, 4, entry, 0)
        for o in range(NO):
            for r in range(8):
                pieces[p, o, r] = totals[o, pl.ds(r, 16, stride=8), :].astype(BF)
        send_x(p)
        if p >= 1:
            send_y(p - 1, 1)
            send_y(p - 1, 3)
        if p >= 2:
            forward(p - 2, 0, 1, 3)

    rho = lax.broadcasted_iota(jnp.int32, (256, 128), 0)
    key = (rho // 16) * 64 + y * 16 + rho % 16
    lane = lax.broadcasted_iota(jnp.int32, (256, 128), 1)

    def node_sums(p):
        for h in range(4):
            for s in range(NY):
                hit = (key == idy[s, p:p + 1, :]) & (lane % 4 == h)
                select[h, :, s * 128:(s + 1) * 128] = jnp.where(hit, 1.0, 0.0).astype(BF)
        for e in range(4):
            f_copies[p, e].wait_recv()

        def two_rows(r, carry):
            lo = rows[:, p, :, 2 * r].reshape(512, 128)
            hi = rows[:, p, :, 2 * r + 1].reshape(512, 128)
            both = jnp.concatenate([lo, hi], axis=1)
            for h in range(4):
                new = mm(select[h], both)
                if p > 0:
                    new = new + acc[h, r]
                if p < NP - 1:
                    acc[h, r] = new
                else:
                    new = new.astype(BF)
                    part[:, h * 8 + 2 * r] = new[:, 0:128].reshape(NZ, 16, 128)
                    part[:, h * 8 + 2 * r + 1] = new[:, 128:256].reshape(NZ, 16, 128)
            return carry

        lax.fori_loop(0, 4, two_rows, 0)

    for copy in iy_copies:
        copy.wait()
    send_y(3, 0)
    send_y(2, 2)
    node_sums(0)
    for e in (1, 3, 2):
        send_y(3, e)
    forward(1, 2)
    forward(2, 0, 1, 3, 2)
    node_sums(1)
    forward(3, 0, 1, 3, 2)
    node_sums(2)
    node_sums(3)

    width = 32 // SUBS
    up_copies, down_copies = {}, {}
    for s in range(8):
        high = lax.rem(z + 8 - s, NZ)
        low = lax.rem(z + NZ - 7 + s, NZ)
        for u in range(SUBS):
            span = pl.ds(u * width, width)
            if s > 0:
                up_copies[s - 1, u].wait_recv()
                part[high, span] = part[high, span] + from_low[s - 1, span]
            up_copies[s, u] = remote(
                part.at[high, span], from_low.at[s, span], ps.at[s, u], pr.at[s, u], up_z
            )
            if s < 7:
                if s > 0:
                    down_copies[s - 1, u].wait_recv()
                    part[low, span] = part[low, span] + from_high[s - 1, span]
                down_copies[s, u] = remote(
                    part.at[low, span], from_high.at[s, span], ms.at[s, u], mr.at[s, u], down_z
                )
    row, col = iotas(256, 256)
    source_lane = (col % 16) // 8 * 128 + (col // 16) * 8 + col % 8
    perm = jnp.where(row == source_lane, 1.0, 0.0).astype(BF)
    for u in range(SUBS):
        down_copies[6, u].wait_recv()
        up_copies[7, u].wait_recv()
    for u in range(16):
        pair = []
        for wh in range(2):
            r = wh * 16 + u
            pair.append((
                part[z, r].astype(F32) + from_low[7, r].astype(F32) + from_high[6, r].astype(F32)
            ).astype(BF))
        out_ref[:, u * 256:(u + 1) * 256] = mm(
            jnp.concatenate(pair, axis=1), perm
        ).astype(BF)
    for copy in list(up_copies.values()) + list(down_copies.values()):
        copy.wait_send()
    for p in range(NP):
        for e in range(4):
            f_copies[p, e].wait_send()
            for copy in y_copies[p, e]:
                copy.wait_send()
        for hop in hops:
            x_copies[p, hop[0], hop[1]].wait_send()


def apply_all(slots, kinds, leaves, nodes, child_cubes, table, two_scale):
    dma = pltpu.SemaphoreType.DMA
    smem = pl.BlockSpec(memory_space=pltpu.SMEM)
    return pl.pallas_call(
        apply_all_kernel,
        out_shape=jax.ShapeDtypeStruct((16, 4096), BF),
        in_specs=[smem] * 4 + [VM] * 3,
        out_specs=VM,
        scratch_shapes=[
            pltpu.VMEM((NO, NP, 16, 256), BF),
            pltpu.VMEM((NO, NP, 16, 256), BF),
            pltpu.VMEM((256, 256), BF),
            pltpu.VMEM((256, 256), BF),
            pltpu.VMEM((32, 32), BF),
            pltpu.VMEM((64, 32), BF),
            pltpu.VMEM((128, 1024), BF),
            pltpu.VMEM((320, 320), BF),
            pltpu.VMEM((960, 32), F32),
            pltpu.VMEM((16, 320, 32), BF),
            pltpu.VMEM((16, 32, 2560), BF),
            pltpu.VMEM((16, 64, 2560), BF),
            pltpu.VMEM((320, 1024), BF),
            pltpu.VMEM((128, 2560), BF),
            pltpu.VMEM((2560, 256), BF),
            pltpu.VMEM((NO, 128, 128), F32),
            pltpu.VMEM((NP, NO, 8, 16, 128), BF),
            pltpu.VMEM((NY, NP, NO, 8, 16, 128), BF),
            pltpu.VMEM((NO, 8, 128), jnp.int32),
            pltpu.VMEM((NY, 8, 128), jnp.int32),
            pltpu.VMEM((4, 256, 512), BF),
            pltpu.VMEM((4, 4, 256, 256), F32),
            pltpu.VMEM((NZ, 32, 16, 128), BF),
            pltpu.VMEM((8, 32, 16, 128), BF),
            pltpu.VMEM((7, 32, 16, 128), BF),
            dma((4, 2)), dma((4, 2)), dma((NP, 4, 2)), dma((NP, 4, 2)), dma((4, 2)), dma((4, 2)),
            dma((2, NP, 4)), dma((2, NP, 4)), dma((NP, 4)), dma((NP, 4)), dma((NY,)), dma((NY,)),
            dma((8, SUBS)), dma((8, SUBS)), dma((7, SUBS)), dma((7, SUBS)),
        ],
        compiler_params=pltpu.CompilerParams(
            collective_id=0, has_side_effects=True, vmem_limit_bytes=56 << 20
        ),
        name="apply_all",
    )(slots, kinds, leaves, nodes, child_cubes, table, two_scale)


def local(children, child_slot, two_scale, factors, disp_kind, target_leaf, target_node):
    out = apply_all(
        child_slot, disp_kind, target_leaf[:, :, 0], target_node,
        children.reshape(32, 16, 256), factors.reshape(-1, 240, 128), two_scale,
    )
    return out.reshape(16, 1, 4096)


def solution(mesh):
    placed = (
        P(("leaf", "oct"), None),
        P("leaf", "oct"),
        P(),
        P(),
        P(("leaf", "oct"), None),
        P(("leaf", "oct"), None, None),
        P(("leaf", "oct"), None),
    )
    return jax.shard_map(
        local, mesh=mesh, in_specs=placed, out_specs=P("leaf", "oct", None), check_vma=False
    )
```

```python
import functools

import jax
import jax.numpy as jnp
from jax import lax
from jax.experimental import pallas as pl
from jax.experimental.pallas import tpu as pltpu
from jax.sharding import PartitionSpec as P

BF = jnp.bfloat16
F32 = jnp.float32
MESH = pl.DeviceIdType.MESH
VM = pl.BlockSpec(memory_space=pltpu.VMEM)
NT = (((1,), (1,)), ((), ()))
NN = (((1,), (0,)), ((), ()))
NY, NZ, NO = 4, 16, 8
SUBS = 2
NP = 4


def mm(a, b, dims=NN):
    return lax.dot_general(a, b, dims, preferred_element_type=F32)


def one_hot(hit):
    return jnp.where(hit, 1.0, 0.0).astype(BF)


def iotas(rows, cols):
    return (
        lax.broadcasted_iota(jnp.int32, (rows, cols), 0),
        lax.broadcasted_iota(jnp.int32, (rows, cols), 1),
    )


def apply_all_kernel(
    slot_ref, kind_ref, leaf_ref, node_ref, ch_ref, tab_ref, w_ref, out_ref,
    stage, blocks, mask2, mask3, wt, wtd, wc4, bd, flat, h0s, base2, base3, s1, lhs3, e3,
    totals, pieces, rows, idx, idy, select, acc, part, from_low, from_high,
    es, er, xs, xr, ixs, ixr, ys, yr, fs, fr, iys, iyr, ps, pr, ms, mr,
):
    leaf, octant = lax.axis_index("leaf"), lax.axis_index("oct")
    z, y = leaf // NY, lax.rem(leaf, NY)
    chip, core = octant // 2, lax.rem(octant, 2)

    def at_y(d):
        return (z * NY + lax.rem(y + d, NY), octant)

    up_z = (lax.rem(z + 1, NZ) * NY + y, octant)
    down_z = (lax.rem(z + NZ - 1, NZ) * NY + y, octant)
    hops = [(2, 0), (2, 1), (1, 0), (1, 1), (3, 0), (3, 1), (0, 1)]
    target = {(e, c): lax.rem(chip + e, 4) * 2 + lax.rem(core + c, 2) for e, c in hops}

    def remote(src, dst, ss, rs, where):
        copy = pltpu.make_async_remote_copy(
            src_ref=src, dst_ref=dst, send_sem=ss, recv_sem=rs, device_id=where,
            device_id_type=MESH,
        )
        copy.start()
        return copy

    barrier = pltpu.get_barrier_semaphore()
    partners = [(leaf, target[hop]) for hop in hops]
    partners += [at_y(1), at_y(2), at_y(3), up_z, down_z]
    for partner in partners:
        pl.semaphore_signal(barrier, inc=1, device_id=partner, device_id_type=MESH)
    for q in range(32):
        stage[q // 4, q % 4] = ch_ref[slot_ref[q, 0]]
    row, col = iotas(8, 128)
    goal = jnp.zeros((8, 128), jnp.int32)
    for p in range(NP):
        for k in range(4):
            goal = jnp.where(
                (row == p) & (col % 16 // 4 == k), leaf_ref[p, k] * 16 + node_ref[p, k], goal
            )
    idx[octant] = jnp.where(col // 16 == octant, goal, 0)
    pl.semaphore_wait(barrier, len(partners))

    e_copies, ix_copies = [], []
    for e, c in hops:
        to = target[e, c]
        e_copies.append(
            remote(stage.at[to], blocks.at[octant], es.at[e, c], er.at[e, c], (leaf, to))
        )
    for e, c in hops:
        to = target[e, c]
        ix_copies.append(
            remote(idx.at[octant], idx.at[octant], ixs.at[e, c], ixr.at[e, c], (leaf, to))
        )
    blocks[octant] = stage[octant]

    w = w_ref[...]
    row, col = iotas(256, 256)
    mask2[...] = one_hot(col % 8 == (row // 16) % 8)
    mask3[...] = one_hot(col % 8 == (row // 8) % 8)
    row, col = iotas(32, 32)
    wt[...] = mm(one_hot(row == col), w, NT).astype(BF)
    row, col = iotas(64, 32)
    wtd[...] = mm(one_hot(col == row // 16 * 8 + row % 8), w, NT).astype(BF)
    row, col = iotas(320, 32)
    tile = one_hot(row % 32 == col)
    row, col = iotas(32, 1024)
    wide = mm(w, one_hot(col % 256 // 8 == row)).astype(BF)
    row, col = iotas(128, 1024)
    wc4[...] = jnp.where(row // 32 == col // 256, mm(tile[0:128], wide), 0.0).astype(BF)
    row, col = iotas(320, 320)
    tall = mm(tile, w, NT).astype(BF)
    bd[...] = jnp.where(row // 32 == col // 32, mm(tall, tile, NT), 0.0).astype(BF)

    def fold(p, k):
        n = p * 4 + k
        dense = tab_ref[kind_ref[p, k]].astype(F32)
        for o in range(4):
            flat[pl.ds(o, 240, stride=4), :] = dense[:, o * 32:(o + 1) * 32]
        g0 = mm(flat[0:320, :].astype(BF), w_ref[...]).astype(BF)
        h0s[n] = mm(bd[...], g0).astype(BF)
        a1 = mm(wtd[...], flat[320:640, :].astype(BF), NT).astype(BF)
        a2 = mm(wt[...], flat[640:960, :].astype(BF), NT).astype(BF)
        for g, width in ((0, 128), (1, 128), (2, 64)):
            ins = slice(g * 128, g * 128 + width)
            outs = slice(g * 1024, g * 1024 + width * 8)
            base3[n, :, outs] = mm(a1[:, ins], wc4[0:width, 0:width * 8]).astype(BF)
            base2[n, :, outs] = mm(a2[:, ins], wc4[0:width, 0:width * 8]).astype(BF)

    def fold_first(k, carry):
        fold(0, k)
        return carry

    lax.fori_loop(0, 4, fold_first, 0)
    for copy in e_copies:
        copy.wait()

    x_copies, y_copies, f_copies = {}, {}, {}

    def send_x(p):
        rows[y, p, octant] = pieces[p, octant]
        for e, c in hops:
            to = target[e, c]
            x_copies[p, e, c] = remote(
                pieces.at[p, to], rows.at[y, p, octant], xs.at[p, e, c], xr.at[p, e, c],
                (leaf, to),
            )

    def pair_of(e):
        return pl.ds(lax.rem(chip + 4 - e, 4) * 2, 2)

    def rows_of(p, half):
        return pl.ds(0, 8) if p < 2 else pl.ds(half * 4, 4)

    def send_y(p, half, *which):
        for e in which:
            for c in range(2):
                if half == 0 and (e, c) != (0, 0):
                    x_copies[p, e, c].wait_recv()
            block = rows.at[y, p, pair_of(e), rows_of(p, half)]
            y_copies[p, e, half] = (
                remote(block, block, ys.at[0, half, p, e], yr.at[0, half, p, e], at_y(1)),
                remote(block, block, ys.at[1, half, p, e], yr.at[1, half, p, e], at_y(3)),
            )

    def forward(p, half, *which):
        for e in which:
            up, down = y_copies[p, e, half]
            up.wait_recv()
            down.wait_recv()
            came, to = (NY - 1, 1) if e < 2 else (1, 3)
            block = rows.at[lax.rem(y + came, NY), p, pair_of(e), rows_of(p, half)]
            f_copies[p, e, half] = remote(
                block, block, fs.at[half, p, e], fr.at[half, p, e], at_y(to)
            )

    iy_copies = []
    for p in range(NP):
        x_rows = []
        for i in range(2):
            tiles = []
            for j in range(2):
                for vh in range(2):
                    for l in range(2):
                        tiles.append(blocks[4 * i + 2 * j + l, p, :, vh * 128:(vh + 1) * 128])
            x_rows.append(jnp.concatenate(tiles, axis=1))
        x = jnp.concatenate(x_rows, axis=0)

        def entry(k, carry):
            n = p * 4 + k
            s1[...] = mm(h0s[n], x).astype(BF)
            for t in range(10):
                lanes = slice(t * 256, (t + 1) * 256)
                for bh in range(4):
                    tile = base3[n, bh * 16:(bh + 1) * 16, lanes]
                    for cp in range(4):
                        r = bh * 64 + cp * 16
                        e3[t * 256 + r:t * 256 + r + 16, :] = tile * mask3[r:r + 16, :]
                low, high = base2[n, 0:16, lanes], base2[n, 16:32, lanes]
                e2 = jnp.concatenate([low] * 8 + [high] * 8, axis=0) * mask2[...]
                lhs2 = jnp.concatenate(
                    [s1[t * 32:(t + 1) * 32, bh * 256:(bh + 1) * 256] for bh in range(4)], axis=0
                )
                mid = mm(lhs2, e2)
                for ch in range(4):
                    lhs3[ch * 32:(ch + 1) * 32, lanes] = jnp.concatenate(
                        [mid[bh * 32:(bh + 1) * 32, ch * 64:(ch + 1) * 64] for bh in range(4)],
                        axis=1,
                    ).astype(BF)
            total = mm(lhs3[...], e3[...])
            for i in range(2):
                for j in range(2):
                    for l in range(2):
                        for wh in range(2):
                            r = (2 * l + wh) * 32 + i * 16
                            start = pl.multiple_of(k * 32 + wh * 16, 16)
                            totals[4 * i + 2 * j + l, pl.ds(start, 16), :] = total[
                                r:r + 16, j * 128:(j + 1) * 128
                            ]
            if p < NP - 1:
                fold(p + 1, k)
            return carry

        lax.fori_loop(0, 2, entry, 0)
        if p == 0:
            for copy in ix_copies:
                copy.wait()
            idy[y] = jnp.sum(idx[...], axis=0)
            for d in range(1, NY):
                iy_copies.append(remote(idy.at[y], idy.at[y], iys.at[d], iyr.at[d], at_y(d)))
        else:
            send_y(p - 1, 0, 0)
        if p >= 2:
            send_y(p - 2, 0, 2)
        if p >= 3:
            forward(p - 3, 0, 2)
        lax.fori_loop(2, 4, entry, 0)
        for o in range(NO):
            for r in range(8):
                pieces[p, o, r] = totals[o, pl.ds(r, 16, stride=8), :].astype(BF)
        send_x(p)
        if p >= 1:
            send_y(p - 1, 0, 1, 3)
        if p >= 2:
            forward(p - 2, 0, 0, 1, 3)

    rho = lax.broadcasted_iota(jnp.int32, (256, 128), 0)
    key = (rho // 16) * 64 + y * 16 + rho % 16
    lane = lax.broadcasted_iota(jnp.int32, (256, 128), 1)

    def node_sums(p, half):
        if half == 0:
            for h in range(4):
                for q in range(NY):
                    hit = (key == idy[q, p:p + 1, :]) & (lane % 4 == h)
                    select[p, h, :, q * 128:(q + 1) * 128] = one_hot(hit)
        for e in range(4):
            f_copies[p, e, half].wait_recv()

        def two_rows(r, carry):
            lo = rows[:, p, :, 2 * r].reshape(512, 128)
            hi = rows[:, p, :, 2 * r + 1].reshape(512, 128)
            both = jnp.concatenate([lo, hi], axis=1)
            for h in range(4):
                new = mm(select[p, h], both)
                if p > 0:
                    new = new + acc[h, r]
                if p < NP - 1:
                    acc[h, r] = new
                else:
                    new = new.astype(BF)
                    at = half * 16 + h * 4 + 2 * (r - 2 * half)
                    part[:, at] = new[:, 0:128].reshape(NZ, 16, 128)
                    part[:, at + 1] = new[:, 128:256].reshape(NZ, 16, 128)
            return carry

        if p < 2:
            lax.fori_loop(0, 4, two_rows, 0)
        else:
            lax.fori_loop(2 * half, 2 * half + 2, two_rows, 0)

    width = 16 // SUBS
    up_copies, down_copies = {}, {}

    def ring(s, half):
        high = lax.rem(z + 8 - s, NZ)
        low = lax.rem(z + NZ - 7 + s, NZ)
        for u in range(half * SUBS, (half + 1) * SUBS):
            span = pl.ds(u * width, width)
            if s > 0:
                up_copies[s - 1, u].wait_recv()
                part[high, span] = part[high, span] + from_low[s - 1, span]
            up_copies[s, u] = remote(
                part.at[high, span], from_low.at[s, span], ps.at[s, u], pr.at[s, u], up_z
            )
            if s < 7:
                if s > 0:
                    down_copies[s - 1, u].wait_recv()
                    part[low, span] = part[low, span] + from_high[s - 1, span]
                down_copies[s, u] = remote(
                    part.at[low, span], from_high.at[s, span], ms.at[s, u], mr.at[s, u], down_z
                )

    row, col = iotas(256, 256)
    source_lane = (col % 16) // 8 * 128 + (col // 16) * 8 + col % 8
    mask2[...] = one_hot(row == source_lane)

    def finish(half):
        for u in range(half * SUBS, (half + 1) * SUBS):
            down_copies[6, u].wait_recv()
            up_copies[7, u].wait_recv()
        for u in range(16):
            if u % 8 // 4 != half:
                continue
            pair = []
            for wh in range(2):
                r = half * 16 + (wh * 2 + u // 8) * 4 + u % 4
                pair.append((
                    part[z, r].astype(F32)
                    + from_low[7, r].astype(F32)
                    + from_high[6, r].astype(F32)
                ).astype(BF))
            out_ref[:, u * 256:(u + 1) * 256] = mm(
                jnp.concatenate(pair, axis=1), mask2[...]
            ).astype(BF)

    for copy in iy_copies:
        copy.wait()
    send_y(2, 0, 2)
    send_y(3, 0, 0)
    node_sums(0, 0)
    send_y(3, 0, 1, 3, 2)
    forward(1, 0, 2)
    forward(2, 0, 0, 1, 3, 2)
    send_y(2, 1, 0, 1, 3, 2)
    node_sums(1, 0)
    forward(3, 0, 0, 1, 3, 2)
    send_y(3, 1, 0, 1, 3, 2)
    node_sums(2, 0)
    forward(2, 1, 0, 1, 3, 2)
    node_sums(3, 0)
    ring(0, 0)
    ring(1, 0)
    forward(3, 1, 0, 1, 3, 2)
    ring(2, 0)
    node_sums(2, 1)
    ring(3, 0)
    node_sums(3, 1)
    ring(0, 1)
    for s in range(4, 8):
        ring(s, 0)
        ring(s - 3, 1)
    ring(5, 1)
    finish(0)
    ring(6, 1)
    ring(7, 1)
    finish(1)
    for copy in list(up_copies.values()) + list(down_copies.values()):
        copy.wait_send()
    for p in range(NP):
        for e in range(4):
            for half in range(1 if p < 2 else 2):
                f_copies[p, e, half].wait_send()
                for copy in y_copies[p, e, half]:
                    copy.wait_send()
        for hop in hops:
            x_copies[p, hop[0], hop[1]].wait_send()


def apply_all(slots, kinds, leaves, nodes, child_cubes, table, two_scale):
    dma = pltpu.SemaphoreType.DMA
    smem = pl.BlockSpec(memory_space=pltpu.SMEM)
    return pl.pallas_call(
        apply_all_kernel,
        out_shape=jax.ShapeDtypeStruct((16, 4096), BF),
        in_specs=[smem] * 4 + [VM] * 3,
        out_specs=VM,
        scratch_shapes=[
            pltpu.VMEM((NO, NP, 16, 256), BF),
            pltpu.VMEM((NO, NP, 16, 256), BF),
            pltpu.VMEM((256, 256), BF),
            pltpu.VMEM((256, 256), BF),
            pltpu.VMEM((32, 32), BF),
            pltpu.VMEM((64, 32), BF),
            pltpu.VMEM((128, 1024), BF),
            pltpu.VMEM((320, 320), BF),
            pltpu.VMEM((960, 32), F32),
            pltpu.VMEM((16, 320, 32), BF),
            pltpu.VMEM((16, 32, 2560), BF),
            pltpu.VMEM((16, 64, 2560), BF),
            pltpu.VMEM((320, 1024), BF),
            pltpu.VMEM((128, 2560), BF),
            pltpu.VMEM((2560, 256), BF),
            pltpu.VMEM((NO, 128, 128), F32),
            pltpu.VMEM((NP, NO, 8, 16, 128), BF),
            pltpu.VMEM((NY, NP, NO, 8, 16, 128), BF),
            pltpu.VMEM((NO, 8, 128), jnp.int32),
            pltpu.VMEM((NY, 8, 128), jnp.int32),
            pltpu.VMEM((NP, 4, 256, 512), BF),
            pltpu.VMEM((4, 4, 256, 256), F32),
            pltpu.VMEM((NZ, 32, 16, 128), BF),
            pltpu.VMEM((8, 32, 16, 128), BF),
            pltpu.VMEM((7, 32, 16, 128), BF),
            dma((4, 2)), dma((4, 2)), dma((NP, 4, 2)), dma((NP, 4, 2)), dma((4, 2)), dma((4, 2)),
            dma((2, 2, NP, 4)), dma((2, 2, NP, 4)), dma((2, NP, 4)), dma((2, NP, 4)),
            dma((NY,)), dma((NY,)),
            dma((8, 2 * SUBS)), dma((8, 2 * SUBS)), dma((7, 2 * SUBS)), dma((7, 2 * SUBS)),
        ],
        compiler_params=pltpu.CompilerParams(
            collective_id=0, has_side_effects=True, vmem_limit_bytes=56 << 20
        ),
        name="apply_all",
    )(slots, kinds, leaves, nodes, child_cubes, table, two_scale)


def local(children, child_slot, two_scale, factors, disp_kind, target_leaf, target_node):
    out = apply_all(
        child_slot, disp_kind, target_leaf[:, :, 0], target_node,
        children.reshape(32, 16, 256), factors.reshape(-1, 240, 128), two_scale,
    )
    return out.reshape(16, 1, 4096)


def solution(mesh):
    placed = (
        P(("leaf", "oct"), None),
        P("leaf", "oct"),
        P(),
        P(),
        P(("leaf", "oct"), None),
        P(("leaf", "oct"), None, None),
        P(("leaf", "oct"), None),
    )
    return jax.shard_map(
        local, mesh=mesh, in_specs=placed, out_specs=P("leaf", "oct", None), check_vma=False
    )
```

```python
import functools

import jax
import jax.numpy as jnp
from jax import lax
from jax.experimental import pallas as pl
from jax.experimental.pallas import tpu as pltpu
from jax.sharding import PartitionSpec as P

BF = jnp.bfloat16
F32 = jnp.float32
MESH = pl.DeviceIdType.MESH
VM = pl.BlockSpec(memory_space=pltpu.VMEM)
NT = (((1,), (1,)), ((), ()))
NN = (((1,), (0,)), ((), ()))
NY, NZ, NO = 4, 16, 8
SUBS = 4
NP = 4


def mm(a, b, dims=NN):
    return lax.dot_general(a, b, dims, preferred_element_type=F32)


def one_hot(hit):
    return jnp.where(hit, 1.0, 0.0).astype(BF)


def iotas(rows, cols):
    return (
        lax.broadcasted_iota(jnp.int32, (rows, cols), 0),
        lax.broadcasted_iota(jnp.int32, (rows, cols), 1),
    )


def apply_all_kernel(
    slot_ref, kind_ref, leaf_ref, node_ref, ch_ref, tab_ref, w_ref, out_ref,
    stage, blocks, mask2, mask3, wt, wtd, wc4, bd, flat, h0s, base2, base3, s1, lhs3, e3,
    totals, pieces, rows, idx, idy, select, acc, part, from_low, from_high,
    es, er, xs, xr, ixs, ixr, ys, yr, fs, fr, iys, iyr, ps, pr, ms, mr,
):
    leaf, octant = lax.axis_index("leaf"), lax.axis_index("oct")
    z, y = leaf // NY, lax.rem(leaf, NY)
    chip, core = octant // 2, lax.rem(octant, 2)

    def at_y(d):
        return (z * NY + lax.rem(y + d, NY), octant)

    up_z = (lax.rem(z + 1, NZ) * NY + y, octant)
    down_z = (lax.rem(z + NZ - 1, NZ) * NY + y, octant)
    hops = [(0, 1), (1, 0), (1, 1), (3, 0), (3, 1), (2, 0), (2, 1)]
    target = {(e, c): lax.rem(chip + e, 4) * 2 + lax.rem(core + c, 2) for e, c in hops}

    def remote(src, dst, ss, rs, where):
        copy = pltpu.make_async_remote_copy(
            src_ref=src, dst_ref=dst, send_sem=ss, recv_sem=rs, device_id=where,
            device_id_type=MESH,
        )
        copy.start()
        return copy

    barrier = pltpu.get_barrier_semaphore()
    partners = [(leaf, target[hop]) for hop in hops]
    partners += [at_y(1), at_y(2), at_y(3), up_z, down_z]
    for partner in partners:
        pl.semaphore_signal(barrier, inc=1, device_id=partner, device_id_type=MESH)
    for q in range(32):
        stage[q // 4, q % 4] = ch_ref[slot_ref[q]]
    row, col = iotas(8, 128)
    goal = jnp.zeros((8, 128), jnp.int32)
    for p in range(NP):
        for k in range(4):
            goal = jnp.where(
                (row == p) & (col % 16 // 4 == k), leaf_ref[p, k] * 16 + node_ref[p, k], goal
            )
    idx[octant] = jnp.where(col // 16 == octant, goal, 0)
    pl.semaphore_wait(barrier, len(partners))

    e_copies, ix_copies = [], []
    for e, c in hops:
        to = target[e, c]
        e_copies.append(
            remote(stage.at[to], blocks.at[octant], es.at[e, c], er.at[e, c], (leaf, to))
        )
    for e, c in hops:
        to = target[e, c]
        ix_copies.append(
            remote(idx.at[octant], idx.at[octant], ixs.at[e, c], ixr.at[e, c], (leaf, to))
        )
    blocks[octant] = stage[octant]

    w = w_ref[...]
    row, col = iotas(256, 256)
    mask2[...] = one_hot(col % 8 == (row // 16) % 8)
    mask3[...] = one_hot(col % 8 == (row // 8) % 8)
    row, col = iotas(32, 32)
    wt[...] = mm(one_hot(row == col), w, NT).astype(BF)
    row, col = iotas(64, 32)
    wtd[...] = mm(one_hot(col == row // 16 * 8 + row % 8), w, NT).astype(BF)
    row, col = iotas(320, 32)
    tile = one_hot(row % 32 == col)
    row, col = iotas(32, 1024)
    wide = mm(w, one_hot(col % 256 // 8 == row)).astype(BF)
    row, col = iotas(128, 1024)
    wc4[...] = jnp.where(row // 32 == col // 256, mm(tile[0:128], wide), 0.0).astype(BF)
    row, col = iotas(320, 320)
    tall = mm(tile, w, NT).astype(BF)
    bd[...] = jnp.where(row // 32 == col // 32, mm(tall, tile, NT), 0.0).astype(BF)

    def fold(p, k):
        n = p * 4 + k
        dense = tab_ref[kind_ref[n // 4, n % 4]].astype(F32)
        for o in range(4):
            flat[pl.ds(o, 240, stride=4), :] = dense[:, o * 32:(o + 1) * 32]
        g0 = mm(flat[0:320, :].astype(BF), w_ref[...]).astype(BF)
        h0s[n] = mm(bd[...], g0).astype(BF)
        a1 = mm(wtd[...], flat[320:640, :].astype(BF), NT).astype(BF)
        a2 = mm(wt[...], flat[640:960, :].astype(BF), NT).astype(BF)
        for g, width in ((0, 128), (1, 128), (2, 64)):
            ins = slice(g * 128, g * 128 + width)
            outs = slice(g * 1024, g * 1024 + width * 8)
            base3[n, :, outs] = mm(a1[:, ins], wc4[0:width, 0:width * 8]).astype(BF)
            base2[n, :, outs] = mm(a2[:, ins], wc4[0:width, 0:width * 8]).astype(BF)

    def fold_first(k, carry):
        fold(0, k)
        return carry

    lax.fori_loop(0, 8, fold_first, 0)
    for copy in e_copies:
        copy.wait()

    x_copies, y_copies, f_copies = {}, {}, {}

    def send_x(p):
        rows[y, p, octant] = pieces[p, octant]
        for e, c in hops:
            to = target[e, c]
            x_copies[p, e, c] = remote(
                pieces.at[p, to], rows.at[y, p, octant], xs.at[p, e, c], xr.at[p, e, c],
                (leaf, to),
            )

    def pair_of(e):
        return pl.ds(lax.rem(chip + 4 - e, 4) * 2, 2)

    def send_y(p, e):
        for c in range(2):
            if (e, c) != (0, 0):
                x_copies[p, e, c].wait_recv()
        block = rows.at[y, p, pair_of(e)]
        y_copies[p, e] = (
            remote(block, block, ys.at[0, p, e], yr.at[0, p, e], at_y(1)),
            remote(block, block, ys.at[1, p, e], yr.at[1, p, e], at_y(3)),
        )

    def forward(p, *which):
        for e in which:
            up, down = y_copies[p, e]
            up.wait_recv()
            down.wait_recv()
            came, to = (NY - 1, 1) if e < 2 else (1, 3)
            block = rows.at[lax.rem(y + came, NY), p, pair_of(e)]
            f_copies[p, e] = remote(block, block, fs.at[p, e], fr.at[p, e], at_y(to))

    iy_copies = []
    for p in range(NP):
        x_rows = []
        for i in range(2):
            tiles = []
            for j in range(2):
                for vh in range(2):
                    for l in range(2):
                        tiles.append(blocks[4 * i + 2 * j + l, p, :, vh * 128:(vh + 1) * 128])
            x_rows.append(jnp.concatenate(tiles, axis=1))
        x = jnp.concatenate(x_rows, axis=0)

        def entry(k, carry):
            n = p * 4 + k
            s1[...] = mm(h0s[n], x).astype(BF)
            for t in range(10):
                lanes = slice(t * 256, (t + 1) * 256)
                for bh in range(4):
                    tile = base3[n, bh * 16:(bh + 1) * 16, lanes]
                    for cp in range(4):
                        r = bh * 64 + cp * 16
                        e3[t * 256 + r:t * 256 + r + 16, :] = tile * mask3[r:r + 16, :]
                low, high = base2[n, 0:16, lanes], base2[n, 16:32, lanes]
                e2 = jnp.concatenate([low] * 8 + [high] * 8, axis=0) * mask2[...]
                lhs2 = jnp.concatenate(
                    [s1[t * 32:(t + 1) * 32, bh * 256:(bh + 1) * 256] for bh in range(4)], axis=0
                )
                mid = mm(lhs2, e2)
                for ch in range(4):
                    lhs3[ch * 32:(ch + 1) * 32, lanes] = jnp.concatenate(
                        [mid[bh * 32:(bh + 1) * 32, ch * 64:(ch + 1) * 64] for bh in range(4)],
                        axis=1,
                    ).astype(BF)
            total = mm(lhs3[...], e3[...])
            for i in range(2):
                for j in range(2):
                    for l in range(2):
                        for wh in range(2):
                            r = (2 * l + wh) * 32 + i * 16
                            start = pl.multiple_of(k * 32 + wh * 16, 16)
                            totals[4 * i + 2 * j + l, pl.ds(start, 16), :] = total[
                                r:r + 16, j * 128:(j + 1) * 128
                            ]
            if 0 < p < NP - 1:
                fold(p + 1, k)
            return carry

        lax.fori_loop(0, 2, entry, 0)
        if p == 0:
            for copy in ix_copies:
                copy.wait()
            idy[y] = jnp.sum(idx[...], axis=0)
            for d in range(1, NY):
                iy_copies.append(remote(idy.at[y], idy.at[y], iys.at[d], iyr.at[d], at_y(d)))
        else:
            send_y(p - 1, 0)
        if p >= 2:
            send_y(p - 2, 2)
        if p >= 3:
            forward(p - 3, 2)
        lax.fori_loop(2, 4, entry, 0)
        for o in range(NO):
            for r in range(8):
                pieces[p, o, r] = totals[o, pl.ds(r, 16, stride=8), :].astype(BF)
        send_x(p)
        if p >= 1:
            send_y(p - 1, 1)
            send_y(p - 1, 3)
        if p >= 2:
            forward(p - 2, 0, 1, 3)

    rho = lax.broadcasted_iota(jnp.int32, (256, 128), 0)
    key = (rho // 16) * 64 + y * 16 + rho % 16
    lane = lax.broadcasted_iota(jnp.int32, (256, 128), 1)

    def node_sums(p):
        for h in range(4):
            for s in range(NY):
                hit = (key == idy[s, p:p + 1, :]) & (lane % 4 == h)
                select[h, :, s * 128:(s + 1) * 128] = jnp.where(hit, 1.0, 0.0).astype(BF)
        for e in range(4):
            f_copies[p, e].wait_recv()

        def two_rows(hs, r):
            lo = rows[:, p, :, 2 * r].reshape(512, 128)
            hi = rows[:, p, :, 2 * r + 1].reshape(512, 128)
            both = jnp.concatenate([lo, hi], axis=1)
            for h in hs:
                new = mm(select[h], both)
                if p > 0:
                    new = new + acc[h, r]
                if p < NP - 1:
                    acc[h, r] = new
                else:
                    new = new.astype(BF)
                    part[:, h * 8 + 2 * r] = new[:, 0:128].reshape(NZ, 16, 128)
                    part[:, h * 8 + 2 * r + 1] = new[:, 128:256].reshape(NZ, 16, 128)

        def all_h(r, carry):
            two_rows(range(4), r)
            return carry

        if p < NP - 1:
            lax.fori_loop(0, 4, all_h, 0)
        else:
            for h in range(4):
                for r in range(4):
                    two_rows((h,), r)
                if h < 2:
                    ring_up(0, h)
                else:
                    ring_down(0, h)

    width = 32 // SUBS
    up_copies, down_copies = {}, {}

    def ring_up(s, u):
        to, span = lax.rem(z + 8 - s, NZ), pl.ds(u * width, width)
        if (s - 1, u) in up_copies:
            up_copies[s - 1, u].wait_recv()
            part[to, span] = part[to, span] + from_low[s - 1, span]
        up_copies[s, u] = remote(
            part.at[to, span], from_low.at[s, span], ps.at[s, u], pr.at[s, u], up_z
        )

    def ring_down(s, u):
        to, span = lax.rem(z + NZ - 8 + s, NZ), pl.ds(u * width, width)
        if (s - 1, u) in down_copies:
            down_copies[s - 1, u].wait_recv()
            part[to, span] = part[to, span] + from_high[s - 1, span]
        down_copies[s, u] = remote(
            part.at[to, span], from_high.at[s, span], ms.at[s, u], mr.at[s, u], down_z
        )

    for copy in iy_copies:
        copy.wait()
    send_y(3, 0)
    send_y(2, 2)
    node_sums(0)
    for e in (1, 3, 2):
        send_y(3, e)
    forward(1, 2)
    forward(2, 0, 1, 3, 2)
    node_sums(1)
    forward(3, 0, 1, 3, 2)
    node_sums(2)
    node_sums(3)

    for s in range(1, 8):
        for u in range(SUBS):
            ring_up(s, u)
            ring_down(s, u)
    row, col = iotas(256, 256)
    source_lane = (col % 16) // 8 * 128 + (col // 16) * 8 + col % 8
    perm = jnp.where(row == source_lane, 1.0, 0.0).astype(BF)
    for u in range(SUBS):
        down_copies[7, u].wait_recv()
        up_copies[7, u].wait_recv()
    for u in range(16):
        pair = []
        for wh in range(2):
            r = wh * 16 + u
            pair.append((
                part[z, r].astype(F32) + from_low[7, r].astype(F32) + from_high[7, r].astype(F32)
            ).astype(BF))
        out_ref[:, u * 256:(u + 1) * 256] = mm(
            jnp.concatenate(pair, axis=1), perm
        ).astype(BF)
    for copy in list(up_copies.values()) + list(down_copies.values()):
        copy.wait_send()
    for p in range(NP):
        for e in range(4):
            f_copies[p, e].wait_send()
            for copy in y_copies[p, e]:
                copy.wait_send()
        for hop in hops:
            x_copies[p, hop[0], hop[1]].wait_send()


def apply_all(slots, kinds, leaves, nodes, child_cubes, table, two_scale):
    dma = pltpu.SemaphoreType.DMA
    smem = pl.BlockSpec(memory_space=pltpu.SMEM)
    return pl.pallas_call(
        apply_all_kernel,
        out_shape=jax.ShapeDtypeStruct((16, 4096), BF),
        in_specs=[smem] * 4 + [VM] * 3,
        out_specs=VM,
        scratch_shapes=[
            pltpu.VMEM((NO, NP, 16, 256), BF),
            pltpu.VMEM((NO, NP, 16, 256), BF),
            pltpu.VMEM((256, 256), BF),
            pltpu.VMEM((256, 256), BF),
            pltpu.VMEM((32, 32), BF),
            pltpu.VMEM((64, 32), BF),
            pltpu.VMEM((128, 1024), BF),
            pltpu.VMEM((320, 320), BF),
            pltpu.VMEM((960, 32), F32),
            pltpu.VMEM((16, 320, 32), BF),
            pltpu.VMEM((16, 32, 2560), BF),
            pltpu.VMEM((16, 64, 2560), BF),
            pltpu.VMEM((320, 1024), BF),
            pltpu.VMEM((128, 2560), BF),
            pltpu.VMEM((2560, 256), BF),
            pltpu.VMEM((NO, 128, 128), F32),
            pltpu.VMEM((NP, NO, 8, 16, 128), BF),
            pltpu.VMEM((NY, NP, NO, 8, 16, 128), BF),
            pltpu.VMEM((NO, 8, 128), jnp.int32),
            pltpu.VMEM((NY, 8, 128), jnp.int32),
            pltpu.VMEM((4, 256, 512), BF),
            pltpu.VMEM((4, 4, 256, 256), F32),
            pltpu.VMEM((NZ, 32, 16, 128), BF),
            pltpu.VMEM((8, 32, 16, 128), BF),
            pltpu.VMEM((8, 32, 16, 128), BF),
            dma((4, 2)), dma((4, 2)), dma((NP, 4, 2)), dma((NP, 4, 2)), dma((4, 2)), dma((4, 2)),
            dma((2, NP, 4)), dma((2, NP, 4)), dma((NP, 4)), dma((NP, 4)), dma((NY,)), dma((NY,)),
            dma((8, SUBS)), dma((8, SUBS)), dma((8, SUBS)), dma((8, SUBS)),
        ],
        compiler_params=pltpu.CompilerParams(
            collective_id=0, has_side_effects=True, vmem_limit_bytes=56 << 20
        ),
        name="apply_all",
    )(slots, kinds, leaves, nodes, child_cubes, table, two_scale)


def local(children, child_slot, two_scale, factors, disp_kind, target_leaf, target_node):
    out = apply_all(
        child_slot.reshape(-1), disp_kind, target_leaf[:, :, 0], target_node,
        children.reshape(32, 16, 256), factors.reshape(-1, 240, 128), two_scale,
    )
    return out.reshape(16, 1, 4096)


def solution(mesh):
    placed = (
        P(("leaf", "oct"), None),
        P("leaf", "oct"),
        P(),
        P(),
        P(("leaf", "oct"), None),
        P(("leaf", "oct"), None, None),
        P(("leaf", "oct"), None),
    )
    return jax.shard_map(
        local, mesh=mesh, in_specs=placed, out_specs=P("leaf", "oct", None), check_vma=False
    )
```

```python
import functools

import jax
import jax.numpy as jnp
from jax import lax
from jax.experimental import pallas as pl
from jax.experimental.pallas import tpu as pltpu
from jax.sharding import PartitionSpec as P

BF = jnp.bfloat16
F32 = jnp.float32
MESH = pl.DeviceIdType.MESH
VM = pl.BlockSpec(memory_space=pltpu.VMEM)
NT = (((1,), (1,)), ((), ()))
NN = (((1,), (0,)), ((), ()))
NY, NZ, NO = 4, 16, 8
SUBS = 4
NP = 4


def mm(a, b, dims=NN):
    return lax.dot_general(a, b, dims, preferred_element_type=F32)


def one_hot(hit):
    return jnp.where(hit, 1.0, 0.0).astype(BF)


def iotas(rows, cols):
    return (
        lax.broadcasted_iota(jnp.int32, (rows, cols), 0),
        lax.broadcasted_iota(jnp.int32, (rows, cols), 1),
    )


def apply_all_kernel(
    slot_ref, kind_ref, leaf_ref, node_ref, ch_ref, tab_ref, w_ref, out_ref,
    stage, blocks, mask2, mask3, wt, wtd, wc4, bd, flat, h0s, base2, base3, s1, lhs3, e3,
    totals, pieces, rows, idx, idy, select, acc, part, from_low, from_high,
    es, er, xs, xr, ixs, ixr, ys, yr, fs, fr, iys, iyr, ps, pr, ms, mr,
):
    leaf, octant = lax.axis_index("leaf"), lax.axis_index("oct")
    z, y = leaf // NY, lax.rem(leaf, NY)
    chip, core = octant // 2, lax.rem(octant, 2)

    def at_y(d):
        return (z * NY + lax.rem(y + d, NY), octant)

    up_z = (lax.rem(z + 1, NZ) * NY + y, octant)
    down_z = (lax.rem(z + NZ - 1, NZ) * NY + y, octant)
    hops = [(0, 1), (1, 0), (1, 1), (3, 0), (3, 1), (2, 0), (2, 1)]
    target = {(e, c): lax.rem(chip + e, 4) * 2 + lax.rem(core + c, 2) for e, c in hops}

    def remote(src, dst, ss, rs, where):
        copy = pltpu.make_async_remote_copy(
            src_ref=src, dst_ref=dst, send_sem=ss, recv_sem=rs, device_id=where,
            device_id_type=MESH,
        )
        copy.start()
        return copy

    barrier = pltpu.get_barrier_semaphore()
    partners = [(leaf, target[hop]) for hop in hops]
    partners += [at_y(1), at_y(2), at_y(3), up_z, down_z]
    for partner in partners:
        pl.semaphore_signal(barrier, inc=1, device_id=partner, device_id_type=MESH)
    for q in range(32):
        stage[q // 4, q % 4] = ch_ref[slot_ref[q]]
    row, col = iotas(8, 128)
    goal = jnp.zeros((8, 128), jnp.int32)
    for p in range(NP):
        for k in range(4):
            goal = jnp.where(
                (row == p) & (col % 16 // 4 == k), leaf_ref[p, k] * 16 + node_ref[p, k], goal
            )
    idx[octant] = jnp.where(col // 16 == octant, goal, 0)
    pl.semaphore_wait(barrier, len(partners))

    e_copies, ix_copies = [], []
    for e, c in hops:
        to = target[e, c]
        e_copies.append(
            remote(stage.at[to], blocks.at[octant], es.at[e, c], er.at[e, c], (leaf, to))
        )
    for e, c in hops:
        to = target[e, c]
        ix_copies.append(
            remote(idx.at[octant], idx.at[octant], ixs.at[e, c], ixr.at[e, c], (leaf, to))
        )
    blocks[octant] = stage[octant]

    w = w_ref[...]
    row, col = iotas(256, 256)
    mask2[...] = one_hot(col % 8 == (row // 16) % 8)
    mask3[...] = one_hot(col % 8 == (row // 8) % 8)
    row, col = iotas(32, 32)
    wt[...] = mm(one_hot(row == col), w, NT).astype(BF)
    row, col = iotas(64, 32)
    wtd[...] = mm(one_hot(col == row // 16 * 8 + row % 8), w, NT).astype(BF)
    row, col = iotas(320, 32)
    tile = one_hot(row % 32 == col)
    row, col = iotas(32, 1024)
    wide = mm(w, one_hot(col % 256 // 8 == row)).astype(BF)
    row, col = iotas(128, 1024)
    wc4[...] = jnp.where(row // 32 == col // 256, mm(tile[0:128], wide), 0.0).astype(BF)
    row, col = iotas(320, 320)
    tall = mm(tile, w, NT).astype(BF)
    bd[...] = jnp.where(row // 32 == col // 32, mm(tall, tile, NT), 0.0).astype(BF)

    def fold(p, k):
        n = p * 4 + k
        dense = tab_ref[kind_ref[n // 4, n % 4]].astype(F32)
        for o in range(4):
            flat[pl.ds(o, 240, stride=4), :] = dense[:, o * 32:(o + 1) * 32]
        g0 = mm(flat[0:320, :].astype(BF), w_ref[...]).astype(BF)
        h0s[n] = mm(bd[...], g0).astype(BF)
        a1 = mm(wtd[...], flat[320:640, :].astype(BF), NT).astype(BF)
        a2 = mm(wt[...], flat[640:960, :].astype(BF), NT).astype(BF)
        for g, width in ((0, 128), (1, 128), (2, 64)):
            ins = slice(g * 128, g * 128 + width)
            outs = slice(g * 1024, g * 1024 + width * 8)
            base3[n, :, outs] = mm(a1[:, ins], wc4[0:width, 0:width * 8]).astype(BF)
            base2[n, :, outs] = mm(a2[:, ins], wc4[0:width, 0:width * 8]).astype(BF)

    def fold_first(k, carry):
        fold(0, k)
        return carry

    lax.fori_loop(0, 8, fold_first, 0)
    for copy in e_copies:
        copy.wait()

    x_copies, y_copies, f_copies = {}, {}, {}

    def send_x(p):
        rows[y, p, octant] = pieces[p, octant]
        for e, c in hops:
            to = target[e, c]
            x_copies[p, e, c] = remote(
                pieces.at[p, to], rows.at[y, p, octant], xs.at[p, e, c], xr.at[p, e, c],
                (leaf, to),
            )

    def pair_of(e):
        return pl.ds(lax.rem(chip + 4 - e, 4) * 2, 2)

    def send_y(p, e):
        for c in range(2):
            if (e, c) != (0, 0):
                x_copies[p, e, c].wait_recv()
        block = rows.at[y, p, pair_of(e)]
        y_copies[p, e] = (
            remote(block, block, ys.at[0, p, e], yr.at[0, p, e], at_y(1)),
            remote(block, block, ys.at[1, p, e], yr.at[1, p, e], at_y(3)),
        )

    def forward(p, *which):
        for e in which:
            up, down = y_copies[p, e]
            (up if e < 2 else down).wait_recv()
            came, to = (NY - 1, 1) if e < 2 else (1, 3)
            block = rows.at[lax.rem(y + came, NY), p, pair_of(e)]
            f_copies[p, e] = remote(block, block, fs.at[p, e], fr.at[p, e], at_y(to))

    iy_copies = []
    for p in range(NP):
        x_rows = []
        for i in range(2):
            tiles = []
            for j in range(2):
                for vh in range(2):
                    for l in range(2):
                        tiles.append(blocks[4 * i + 2 * j + l, p, :, vh * 128:(vh + 1) * 128])
            x_rows.append(jnp.concatenate(tiles, axis=1))
        x = jnp.concatenate(x_rows, axis=0)

        def entry(k, carry):
            n = p * 4 + k
            s1[...] = mm(h0s[n], x).astype(BF)
            for t in range(10):
                lanes = slice(t * 256, (t + 1) * 256)
                for bh in range(4):
                    tile = base3[n, bh * 16:(bh + 1) * 16, lanes]
                    for cp in range(4):
                        r = bh * 64 + cp * 16
                        e3[t * 256 + r:t * 256 + r + 16, :] = tile * mask3[r:r + 16, :]
                low, high = base2[n, 0:16, lanes], base2[n, 16:32, lanes]
                e2 = jnp.concatenate([low] * 8 + [high] * 8, axis=0) * mask2[...]
                lhs2 = jnp.concatenate(
                    [s1[t * 32:(t + 1) * 32, bh * 256:(bh + 1) * 256] for bh in range(4)], axis=0
                )
                mid = mm(lhs2, e2)
                for ch in range(4):
                    lhs3[ch * 32:(ch + 1) * 32, lanes] = jnp.concatenate(
                        [mid[bh * 32:(bh + 1) * 32, ch * 64:(ch + 1) * 64] for bh in range(4)],
                        axis=1,
                    ).astype(BF)
            total = mm(lhs3[...], e3[...])
            for i in range(2):
                for j in range(2):
                    for l in range(2):
                        for wh in range(2):
                            r = (2 * l + wh) * 32 + i * 16
                            start = pl.multiple_of(k * 32 + wh * 16, 16)
                            totals[4 * i + 2 * j + l, pl.ds(start, 16), :] = total[
                                r:r + 16, j * 128:(j + 1) * 128
                            ]
            if 0 < p < NP - 1:
                fold(p + 1, k)
            return carry

        lax.fori_loop(0, 2, entry, 0)
        if p == 0:
            for copy in ix_copies:
                copy.wait()
            idy[y] = jnp.sum(idx[...], axis=0)
            for d in range(1, NY):
                iy_copies.append(remote(idy.at[y], idy.at[y], iys.at[d], iyr.at[d], at_y(d)))
        else:
            send_y(p - 1, 0)
        if p >= 2:
            send_y(p - 2, 2)
        if p >= 3:
            forward(p - 3, 2)
        lax.fori_loop(2, 4, entry, 0)
        for o in range(NO):
            for r in range(8):
                pieces[p, o, r] = totals[o, pl.ds(r, 16, stride=8), :].astype(BF)
        send_x(p)
        if p >= 1:
            send_y(p - 1, 1)
            send_y(p - 1, 3)
        if p >= 2:
            forward(p - 2, 0, 1, 3)

    rho = lax.broadcasted_iota(jnp.int32, (256, 128), 0)
    key = (rho // 16) * 64 + y * 16 + rho % 16
    lane = lax.broadcasted_iota(jnp.int32, (256, 128), 1)

    def node_sums(p):
        for h in range(4):
            for s in range(NY):
                hit = (key == idy[s, p:p + 1, :]) & (lane % 4 == h)
                select[h, :, s * 128:(s + 1) * 128] = jnp.where(hit, 1.0, 0.0).astype(BF)
        for e in range(4):
            y_copies[p, e][1 if e < 2 else 0].wait_recv()
            f_copies[p, e].wait_recv()

        def two_rows(hs, r):
            lo = rows[:, p, :, 2 * r].reshape(512, 128)
            hi = rows[:, p, :, 2 * r + 1].reshape(512, 128)
            both = jnp.concatenate([lo, hi], axis=1)
            for h in hs:
                new = mm(select[h], both)
                if p > 0:
                    new = new + acc[h, r]
                if p < NP - 1:
                    acc[h, r] = new
                else:
                    new = new.astype(BF)
                    part[:, h * 8 + 2 * r] = new[:, 0:128].reshape(NZ, 16, 128)
                    part[:, h * 8 + 2 * r + 1] = new[:, 128:256].reshape(NZ, 16, 128)

        def all_h(r, carry):
            two_rows(range(4), r)
            return carry

        if p < NP - 1:
            lax.fori_loop(0, 4, all_h, 0)
        else:
            for h in range(4):
                for r in range(4):
                    two_rows((h,), r)
                if h < 2:
                    ring_up(0, h)
                else:
                    ring_down(0, h)

    width = 32 // SUBS
    up_copies, down_copies = {}, {}

    def ring_up(s, u):
        to, span = lax.rem(z + 8 - s, NZ), pl.ds(u * width, width)
        if (s - 1, u) in up_copies:
            up_copies[s - 1, u].wait_recv()
            part[to, span] = part[to, span] + from_low[s - 1, span]
        up_copies[s, u] = remote(
            part.at[to, span], from_low.at[s, span], ps.at[s, u], pr.at[s, u], up_z
        )

    def ring_down(s, u):
        to, span = lax.rem(z + NZ - 8 + s, NZ), pl.ds(u * width, width)
        if (s - 1, u) in down_copies:
            down_copies[s - 1, u].wait_recv()
            part[to, span] = part[to, span] + from_high[s - 1, span]
        down_copies[s, u] = remote(
            part.at[to, span], from_high.at[s, span], ms.at[s, u], mr.at[s, u], down_z
        )

    for copy in iy_copies:
        copy.wait()
    send_y(3, 0)
    send_y(2, 2)
    node_sums(0)
    for e in (1, 3, 2):
        send_y(3, e)
    forward(1, 2)
    forward(2, 0, 1, 3, 2)
    node_sums(1)
    forward(3, 0, 1, 3, 2)
    node_sums(2)
    node_sums(3)

    for s in range(1, 8):
        for u in range(SUBS):
            ring_up(s, u)
            ring_down(s, u)
    row, col = iotas(256, 256)
    source_lane = (col % 16) // 8 * 128 + (col // 16) * 8 + col % 8
    perm = jnp.where(row == source_lane, 1.0, 0.0).astype(BF)
    for u in range(SUBS):
        down_copies[7, u].wait_recv()
        up_copies[7, u].wait_recv()
    for u in range(16):
        pair = []
        for wh in range(2):
            r = wh * 16 + u
            pair.append((
                part[z, r].astype(F32) + from_low[7, r].astype(F32) + from_high[7, r].astype(F32)
            ).astype(BF))
        out_ref[:, u * 256:(u + 1) * 256] = mm(
            jnp.concatenate(pair, axis=1), perm
        ).astype(BF)
    for copy in list(up_copies.values()) + list(down_copies.values()):
        copy.wait_send()
    for p in range(NP):
        for e in range(4):
            f_copies[p, e].wait_send()
            for copy in y_copies[p, e]:
                copy.wait_send()
        for hop in hops:
            x_copies[p, hop[0], hop[1]].wait_send()


def apply_all(slots, kinds, leaves, nodes, child_cubes, table, two_scale):
    dma = pltpu.SemaphoreType.DMA
    smem = pl.BlockSpec(memory_space=pltpu.SMEM)
    return pl.pallas_call(
        apply_all_kernel,
        out_shape=jax.ShapeDtypeStruct((16, 4096), BF),
        in_specs=[smem] * 4 + [VM] * 3,
        out_specs=VM,
        scratch_shapes=[
            pltpu.VMEM((NO, NP, 16, 256), BF),
            pltpu.VMEM((NO, NP, 16, 256), BF),
            pltpu.VMEM((256, 256), BF),
            pltpu.VMEM((256, 256), BF),
            pltpu.VMEM((32, 32), BF),
            pltpu.VMEM((64, 32), BF),
            pltpu.VMEM((128, 1024), BF),
            pltpu.VMEM((320, 320), BF),
            pltpu.VMEM((960, 32), F32),
            pltpu.VMEM((16, 320, 32), BF),
            pltpu.VMEM((16, 32, 2560), BF),
            pltpu.VMEM((16, 64, 2560), BF),
            pltpu.VMEM((320, 1024), BF),
            pltpu.VMEM((128, 2560), BF),
            pltpu.VMEM((2560, 256), BF),
            pltpu.VMEM((NO, 128, 128), F32),
            pltpu.VMEM((NP, NO, 8, 16, 128), BF),
            pltpu.VMEM((NY, NP, NO, 8, 16, 128), BF),
            pltpu.VMEM((NO, 8, 128), jnp.int32),
            pltpu.VMEM((NY, 8, 128), jnp.int32),
            pltpu.VMEM((4, 256, 512), BF),
            pltpu.VMEM((4, 4, 256, 256), F32),
            pltpu.VMEM((NZ, 32, 16, 128), BF),
            pltpu.VMEM((8, 32, 16, 128), BF),
            pltpu.VMEM((8, 32, 16, 128), BF),
            dma((4, 2)), dma((4, 2)), dma((NP, 4, 2)), dma((NP, 4, 2)), dma((4, 2)), dma((4, 2)),
            dma((2, NP, 4)), dma((2, NP, 4)), dma((NP, 4)), dma((NP, 4)), dma((NY,)), dma((NY,)),
            dma((8, SUBS)), dma((8, SUBS)), dma((8, SUBS)), dma((8, SUBS)),
        ],
        compiler_params=pltpu.CompilerParams(
            collective_id=0, has_side_effects=True, vmem_limit_bytes=56 << 20
        ),
        name="apply_all",
    )(slots, kinds, leaves, nodes, child_cubes, table, two_scale)


def local(children, child_slot, two_scale, factors, disp_kind, target_leaf, target_node):
    out = apply_all(
        child_slot.reshape(-1), disp_kind, target_leaf[:, :, 0], target_node,
        children.reshape(32, 16, 256), factors.reshape(-1, 240, 128), two_scale,
    )
    return out.reshape(16, 1, 4096)


def solution(mesh):
    placed = (
        P(("leaf", "oct"), None),
        P("leaf", "oct"),
        P(),
        P(),
        P(("leaf", "oct"), None),
        P(("leaf", "oct"), None, None),
        P(("leaf", "oct"), None),
    )
    return jax.shard_map(
        local, mesh=mesh, in_specs=placed, out_specs=P("leaf", "oct", None), check_vma=False
    )
```
